32 devices in a mesh: chan: 4 (over x, core), slab: 8 (over z, y).
Axes of the slice: x: 2, y: 2, z: 4, core: 2. Of those that a mesh axis runs over, the one named last changes fastest.
Arguments:
- image: float32 [4, 1024, 1024], P('chan', 'slab'), may hold values from 0 to 2
- margin: int32 [8], P('slab'), may hold values from 1 to 3
- cells: int32 [4, 32768], P('chan', 'slab'), may hold values from 1 to 131071
- weights: float32 [4, 32768], P('chan', 'slab'), may hold values from 0.25 to 4
- observed: float32 [2, 4, 32768], P(None, 'chan', 'slab'), may hold values from -6 to 6
- dual_start: float32 [2, 4, 32768], P(None, 'chan', 'slab'), may hold values from -4 to 4
Outputs:
- restored: float32 [4, 1024, 1024], P('chan', 'slab')
- vis_dual: float32 [2, 4, 32768], P(None, 'chan', 'slab')
The draws below stay inside these ranges and needn't reach their ends.
Inputs may be any that keep to these rules, and one draw needn't show every extreme that they name: `cells`: visibility k of a channel belongs to facet s = k div 4096; its value q names frequency column s * 128 + q div 1024 and frequency row q mod 1024.
All inputs are finite; a program needn't handle non-finite values.
Results may differ from the reference program's by a relative error of at most 0.0047.
Values may be sent and summed in bfloat16 or wider, within the bound.
A program may use at most 64 MiB of HBM per device.

```python
import math
import jax
import jax.numpy as jnp
from jax import lax

N = 1024
VIS_DEV = 4096
ITERS = 1
HALO = 3
CHANNELS = 4
FACETS = 8
ROWS_DEV = 128
VISIBILITIES = 32768


def place_ends(result, stream_key, smallest, top_value):
    longest = result.shape.index(max(result.shape))
    spots = []
    for shift in (0, 1):
        where = [jax.random.randint(jax.random.fold_in(stream_key, axis), (), 0, length) for axis, length in enumerate(result.shape)]
        where[longest] = (where[longest] + shift) % result.shape[longest]
        spots.append(tuple(where))
    return result.at[spots[0]].set(smallest).at[spots[1]].set(top_value)


def block_scale(key, dims, shards, smallest, high):
    loudness = 1.0
    for dim, blocks in shards:
        steps = jax.random.uniform(jax.random.fold_in(jax.random.fold_in(key, 6), dim), (blocks,), jnp.float32, smallest / len(shards), high / len(shards))
        loudness = loudness * jnp.repeat(jnp.exp(steps), dims[dim] // blocks).reshape((-1,) + (1,) * (len(dims) - 1 - dim))
    return loudness


def scatter_about(stream_key, dims, scale, reach, split=(), kind=jnp.bfloat16):
    level = block_scale(stream_key, dims, split, -0.22, 0.18) if split else 1.0
    entries = jax.random.normal(stream_key, dims, jnp.float32) * scale * level
    return jnp.minimum(jnp.maximum(entries, -reach), reach).astype(kind)


def setup_inputs(seed: int = 0) -> dict:
    splits = jax.random.split(jax.random.key(seed), 7)
    return {
        "image": jnp.clip(2.0 * jax.random.uniform(splits[0], (CHANNELS, N, N), jnp.float32) ** block_scale(splits[0], (CHANNELS, N, N), ((0, 4), (1, 8)), -0.2, 0.2), 0.0, 2.0),
        "margin": place_ends(jax.random.randint(splits[1], (FACETS,), 1, HALO + 1), jax.random.fold_in(splits[1], 1), 1, HALO).astype(jnp.int32),
        "cells": place_ends(jax.random.randint(splits[2], (CHANNELS, VISIBILITIES), 1, ROWS_DEV * N), jax.random.fold_in(splits[2], 1), 1, (ROWS_DEV * N) - 1).astype(jnp.int32),
        "weights": jnp.clip(jnp.exp(math.log(4.0) - 2.7725887 * jax.random.uniform(splits[3], (CHANNELS, VISIBILITIES), jnp.float32) ** block_scale(splits[3], (CHANNELS, VISIBILITIES), ((0, 4), (1, 8)), -0.2, 0.2)), 0.25, 4.0),
        "observed": scatter_about(splits[4], (2, CHANNELS, VISIBILITIES), 1.0, 6.0, ((1, 4), (2, 8)), jnp.float32),
        "dual_start": scatter_about(splits[5], (2, CHANNELS, VISIBILITIES), 0.5, 4.0, ((1, 4), (2, 8)), jnp.float32),
    }


low_taps = (-0.010597401784997278, 0.032883011666982945, 0.030841381835986965, -0.18703481171888114, -0.02798376941698385, 0.6308807679295904, 0.7148465705525415, 0.23037781330885523)
high_taps = (-0.23037781330885523, 0.7148465705525415, -0.6308807679295904, -0.02798376941698385, 0.18703481171888114, 0.030841381835986965, -0.032883011666982945, -0.010597401784997278)
tau_step = 0.5
bound_level = 3.0

def tap_value(offset, taps):
    total = jnp.zeros(offset.shape, jnp.float32)
    for position in range(8):
        total = total + jnp.where(offset == position, taps[position], 0.0).astype(jnp.float32)
    return total

def fourier_tables(length):
    index = jnp.arange(length, dtype=jnp.int32)
    product = index[:, None] * index[None, :] % length
    angle = product.astype(jnp.float32) * (2.0 * math.pi / length)
    scale = 1.0 / math.sqrt(length)
    return ((jnp.cos(angle) * scale).astype(jnp.bfloat16), (jnp.sin(angle) * scale).astype(jnp.bfloat16))

def column_matrix(length):
    half = length // 2
    line = jnp.arange(length, dtype=jnp.int32)[:, None]
    column = jnp.arange(length, dtype=jnp.int32)[None, :]
    offset = line - 2 * (column % half) + HALO
    return jnp.where(column < half, tap_value(offset, low_taps), tap_value(offset, high_taps))

def row_matrix(count):
    half = count // 2
    line = jnp.arange(count + 2 * HALO, dtype=jnp.int32)[:, None]
    column = jnp.arange(count, dtype=jnp.int32)[None, :]
    offset = line - 2 * (column % half)
    return jnp.where(column < half, tap_value(offset, low_taps), tap_value(offset, high_taps))

def facet_mask(count, width):
    line = jnp.arange(count + 2 * HALO, dtype=jnp.int32)
    distance = jnp.maximum(jnp.maximum(HALO - line, line - count - HALO + 1), 0)
    return (distance[None, :] <= width[:, None]).astype(jnp.float32)

def forward_grid(plane, cos_table, sin_table):
    flat_b = plane.astype(jnp.bfloat16)
    spec_real = jnp.dot(flat_b, cos_table, preferred_element_type=jnp.float32).astype(jnp.bfloat16)
    spec_imag = (-jnp.dot(flat_b, sin_table, preferred_element_type=jnp.float32)).astype(jnp.bfloat16)
    grid_real = jnp.dot(spec_real.T, cos_table, preferred_element_type=jnp.float32) + jnp.dot(spec_imag.T, sin_table, preferred_element_type=jnp.float32)
    grid_imag = jnp.dot(spec_imag.T, cos_table, preferred_element_type=jnp.float32) - jnp.dot(spec_real.T, sin_table, preferred_element_type=jnp.float32)
    return (grid_real, grid_imag)

def adjoint_grid(hold_real, hold_imag, cos_table, sin_table):
    back_real = (jnp.dot(hold_real, cos_table, preferred_element_type=jnp.float32) - jnp.dot(hold_imag, sin_table, preferred_element_type=jnp.float32)).astype(jnp.bfloat16)
    back_imag = (jnp.dot(hold_real, sin_table, preferred_element_type=jnp.float32) + jnp.dot(hold_imag, cos_table, preferred_element_type=jnp.float32)).astype(jnp.bfloat16)
    return jnp.dot(back_real.T, cos_table, preferred_element_type=jnp.float32) - jnp.dot(back_imag.T, sin_table, preferred_element_type=jnp.float32)

def accumulate(positions, values):
    return jnp.zeros((N * N,), jnp.float32).at[positions].add(values)

def reference(image, margin, cells, weights, observed, dual_start):
    highest = lax.Precision.HIGHEST
    cos_table, sin_table = fourier_tables(N)
    column_map = column_matrix(N)
    row_map = row_matrix(ROWS_DEV)
    mask = facet_mask(ROWS_DEV, margin)
    index = jnp.arange(FACETS, dtype=jnp.int32)[:, None] * ROWS_DEV + jnp.arange(ROWS_DEV + 2 * HALO, dtype=jnp.int32)[None, :]
    offsets = jnp.arange(VISIBILITIES, dtype=jnp.int32) // VIS_DEV * (ROWS_DEV * N)
    place = (cells + offsets[None, :]).astype(jnp.int32)
    estimate = image
    lifted = image
    vis_dual = dual_start
    wave_dual = jnp.zeros((CHANNELS, FACETS, ROWS_DEV, N), jnp.float32)
    for iteration in range(ITERS):
        grid_real, grid_imag = lax.map(lambda plane: forward_grid(plane, cos_table, sin_table), lifted)
        model_real = weights * jnp.take_along_axis(grid_real.reshape(CHANNELS, N * N), place, axis=1)
        model_imag = weights * jnp.take_along_axis(grid_imag.reshape(CHANNELS, N * N), place, axis=1)
        model = jnp.stack([model_real, model_imag])
        vis_dual = (vis_dual + (model - observed)) / 2.0
        hold_real = jax.vmap(accumulate)(place, weights * vis_dual[0]).reshape(CHANNELS, N, N).astype(jnp.bfloat16)
        hold_imag = jax.vmap(accumulate)(place, weights * vis_dual[1]).reshape(CHANNELS, N, N).astype(jnp.bfloat16)
        data_term = lax.map(lambda pair: adjoint_grid(pair[0], pair[1], cos_table, sin_table), (hold_real, hold_imag))
        padded = jnp.pad(lifted, ((0, 0), (HALO, HALO), (0, 0)))
        extended = padded[:, index, :] * mask[None, :, :, None]
        filtered = jnp.einsum('cfen,nm->cfem', extended, column_map, precision=highest)
        coef = jnp.einsum('er,cfem->cfrm', row_map, filtered, precision=highest)
        mixed = wave_dual + coef
        total = lax.optimization_barrier(jnp.sum(mixed * mixed, axis=0))
        factor = bound_level / jnp.maximum(jnp.sqrt(total), bound_level)
        wave_dual = mixed * factor[None]
        back = jnp.einsum('cfrm,nm->cfrn', wave_dual, column_map, precision=highest)
        spread = jnp.einsum('er,cfrn->cfen', row_map, back, precision=highest) * mask[None, :, :, None]
        target = jnp.zeros((CHANNELS, N + 2 * HALO, N), jnp.float32).at[:, index, :].add(spread)
        wave_term = target[:, HALO:N + HALO, :]
        fresh = jnp.maximum(estimate - tau_step * (data_term + wave_term), 0.0)
        lifted = 2.0 * fresh - estimate
        estimate = fresh
    return (estimate, vis_dual)
```

```python
import functools
import math

import jax
import jax.numpy as jnp
import numpy as np
from jax import lax
from jax.experimental import pallas as pl
from jax.experimental.pallas import tpu as pltpu
from jax.sharding import PartitionSpec as P

N = 1024
HALO = 3


low_taps = (
    -0.010597401784997278,
    0.032883011666982945,
    0.030841381835986965,
    -0.18703481171888114,
    -0.02798376941698385,
    0.6308807679295904,
    0.7148465705525415,
    0.23037781330885523,
)
high_taps = (
    -0.23037781330885523,
    0.7148465705525415,
    -0.6308807679295904,
    -0.02798376941698385,
    0.18703481171888114,
    0.030841381835986965,
    -0.032883011666982945,
    -0.010597401784997278,
)
tau_step = 0.5
bound_level = 3.0
leading = (((0,), (0,)), ((), ()))


def with_halo(block, sides, width):
    for axis, dim in sides:
        count = lax.axis_size(axis)
        forward = [(i, i + 1) for i in range(count - 1)]
        backward = [(target, source) for source, target in forward]
        low = lax.ppermute(
            lax.slice_in_dim(block, block.shape[dim] - width, None, axis=dim), axis, forward
        )
        high = lax.ppermute(lax.slice_in_dim(block, 0, width, axis=dim), axis, backward)
        block = jnp.concatenate([low, block, high], axis=dim)
    return block


def tap_value(offset, taps):
    total = jnp.zeros(offset.shape, jnp.float32)
    for position in range(8):
        total = total + jnp.where(offset == position, taps[position], 0.0).astype(jnp.float32)
    return total


def fourier_tables(length):
    index = jnp.arange(length, dtype=jnp.int32)
    product = index[:, None] * index[None, :] % length
    angle = product.astype(jnp.float32) * (2.0 * math.pi / length)
    scale = 1.0 / math.sqrt(length)
    return (
        (jnp.cos(angle) * scale).astype(jnp.bfloat16),
        (jnp.sin(angle) * scale).astype(jnp.bfloat16),
    )


def row_matrix(count):
    half = count // 2
    line = jnp.arange(count + 2 * HALO, dtype=jnp.int32)[:, None]
    column = jnp.arange(count, dtype=jnp.int32)[None, :]
    offset = line - 2 * (column % half)
    return jnp.where(column < half, tap_value(offset, low_taps), tap_value(offset, high_taps))


def facet_mask(count, width):
    line = jnp.arange(count + 2 * HALO, dtype=jnp.int32)
    distance = jnp.maximum(jnp.maximum(HALO - line, line - count - HALO + 1), 0)
    return (distance[None, :] <= width[:, None]).astype(jnp.float32)


def column_forward(values):
    width = values.shape[1]
    half = width // 2
    padded = jnp.pad(values, ((0, 0), (HALO, 8)))
    even_cells = padded[:, 0::2]
    odd_cells = padded[:, 1::2]
    low_part = jnp.zeros((values.shape[0], half), jnp.float32)
    high_part = jnp.zeros((values.shape[0], half), jnp.float32)
    for position in range(8):
        source = even_cells if position % 2 == 0 else odd_cells
        piece = source[:, position // 2 : position // 2 + half]
        low_part = low_part + low_taps[position] * piece
        high_part = high_part + high_taps[position] * piece
    return jnp.concatenate([low_part, high_part], axis=1)


def column_adjoint(coefs):
    width = coefs.shape[1]
    half = width // 2
    low_part = coefs[:, :half]
    high_part = coefs[:, half:]
    even_sums = jnp.zeros((coefs.shape[0], half + 4), jnp.float32)
    odd_sums = jnp.zeros((coefs.shape[0], half + 4), jnp.float32)
    for position in range(8):
        term = low_taps[position] * low_part + high_taps[position] * high_part
        placed = jnp.pad(term, ((0, 0), (position // 2, 4 - position // 2)))
        if position % 2 == 0:
            even_sums = even_sums + placed
        else:
            odd_sums = odd_sums + placed
    joined = jnp.stack([even_sums, odd_sums], axis=2).reshape(coefs.shape[0], width + 8)
    return joined[:, HALO : HALO + width]


def data_part(lifted, dual, seen, places, gains, cos_table, sin_table):
    flat_b = lifted.astype(jnp.bfloat16)
    spectra = jnp.stack(
        [
            jnp.dot(flat_b, cos_table, preferred_element_type=jnp.float32),
            -jnp.dot(flat_b, sin_table, preferred_element_type=jnp.float32),
        ]
    ).astype(jnp.bfloat16)
    columns = lax.all_to_all(spectra, "slab", split_axis=2, concat_axis=1, tiled=True)
    grid_real = lax.dot_general(
        columns[0], cos_table, leading, preferred_element_type=jnp.float32
    ) + lax.dot_general(columns[1], sin_table, leading, preferred_element_type=jnp.float32)
    grid_imag = lax.dot_general(
        columns[1], cos_table, leading, preferred_element_type=jnp.float32
    ) - lax.dot_general(columns[0], sin_table, leading, preferred_element_type=jnp.float32)
    model = jnp.stack(
        [gains * grid_real.reshape(-1)[places], gains * grid_imag.reshape(-1)[places]]
    )
    fresh_dual = (dual + (model - seen)) / 2.0
    weighted = gains[None, :] * fresh_dual
    cell_count = grid_real.size
    hold_real = (
        jnp.zeros((cell_count,), jnp.float32)
        .at[places]
        .add(weighted[0])
        .reshape(grid_real.shape)
        .astype(jnp.bfloat16)
    )
    hold_imag = (
        jnp.zeros((cell_count,), jnp.float32)
        .at[places]
        .add(weighted[1])
        .reshape(grid_real.shape)
        .astype(jnp.bfloat16)
    )
    backward = jnp.stack(
        [
            jnp.dot(hold_real, cos_table, preferred_element_type=jnp.float32)
            - jnp.dot(hold_imag, sin_table, preferred_element_type=jnp.float32),
            jnp.dot(hold_real, sin_table, preferred_element_type=jnp.float32)
            + jnp.dot(hold_imag, cos_table, preferred_element_type=jnp.float32),
        ]
    ).astype(jnp.bfloat16)
    returned = lax.all_to_all(backward, "slab", split_axis=2, concat_axis=1, tiled=True)
    data_term = lax.dot_general(
        returned[0], cos_table, leading, preferred_element_type=jnp.float32
    ) - lax.dot_general(returned[1], sin_table, leading, preferred_element_type=jnp.float32)
    return (data_term, fresh_dual)


def wave_part(lifted, row_map, mask):
    highest = lax.Precision.HIGHEST
    count = lifted.shape[0]
    extended = with_halo(lifted, (("slab", 0),), HALO) * mask
    filtered = column_forward(extended)
    coef = lax.dot_general(
        row_map, filtered, leading, precision=highest, preferred_element_type=jnp.float32
    )
    squares = coef * coef
    share = lax.psum_scatter(
        squares.astype(jnp.bfloat16), "chan", scatter_dimension=1, tiled=True
    ).astype(jnp.float32)
    partial_factor = bound_level / jnp.maximum(jnp.sqrt(share), bound_level)
    factor = lax.all_gather(partial_factor, "chan", axis=1, tiled=True)
    fresh_dual = coef * factor
    back = column_adjoint(fresh_dual)
    spread = jnp.dot(row_map, back, precision=highest, preferred_element_type=jnp.float32) * mask
    bands = jnp.concatenate([spread[:HALO], spread[count + HALO :]], axis=0)
    arrived = with_halo(bands, (("slab", 0),), HALO)
    inner = spread[HALO : count + HALO]
    inner = inner.at[:HALO].add(arrived[:HALO])
    inner = inner.at[count - HALO :].add(arrived[3 * HALO :])
    return (inner, fresh_dual)


def local_plain(image, margin, cells, weights, observed, dual_start):
    count = image.shape[1]
    cos_table, sin_table = fourier_tables(N)
    row_map = row_matrix(count)
    mask = facet_mask(count, margin)[0][:, None]
    places = cells[0]
    gains = weights[0]
    seen = observed[:, 0, :]
    dual = dual_start[:, 0, :]
    estimate = image[0]
    data_term, dual = data_part(estimate, dual, seen, places, gains, cos_table, sin_table)
    wave_term, wave_dual = wave_part(estimate, row_map, mask)
    fresh = jnp.maximum(estimate - tau_step * (data_term + wave_term), 0.0)
    return (fresh[None], dual[:, None, :])


LANES = 128
EDGE = 8
CHUNK = 512
TILE = 16
highest = lax.Precision.HIGHEST
crossed = (((1,), (1,)), ((), ()))


def pick(offset, taps):
    inside = (offset >= 0) & (offset < 8)
    return np.where(inside, np.asarray(taps, np.float64)[np.clip(offset, 0, 7)], 0.0)


def both_taps(offset, is_low):
    return np.where(is_low, pick(offset, low_taps), pick(offset, high_taps)).astype(np.float32)


def wave_rows(lines, length, span):
    angle = lines[:, None] * np.arange(span)[None, :] % length * (2.0 * np.pi / length)
    scale = 1.0 / np.sqrt(length)
    return np.cos(angle) * scale, -np.sin(angle) * scale


def first_column(owner, n, count):
    return count * owner if owner < n // 2 else count * (n - 1 - owner) + count // 2


def owner_table(n, count, width):
    blocks = []
    for owner in range(n):
        lines = first_column(owner, n, count) + np.arange(count // 2)
        blocks.extend(wave_rows(lines, width, width // 2))
    return np.concatenate(blocks).astype(np.float32).astype(jnp.bfloat16)


def edge_table(n, count, width):
    table = np.zeros((n // 2, TILE, width), np.float32)
    real, imag = wave_rows(count * (1 + np.arange(n // 2)), width, width)
    table[:, 0], table[:, TILE // 2] = real, imag
    return table.reshape(-1, width).astype(jnp.bfloat16)


def analysis_map():
    line = np.arange(4 * LANES)[:, None]
    column = np.arange(2 * LANES)[None, :]
    offset = line - (LANES - HALO) - 2 * (column % LANES)
    return both_taps(offset, column < LANES)


def synthesis_map():
    line = np.arange(6 * LANES)[:, None]
    column = np.arange(2 * LANES)[None, :]
    block = line // (2 * LANES) - 1
    offset = column - 2 * LANES * block - 2 * (line % LANES) + HALO
    return both_taps(offset, line % (2 * LANES) < LANES)


def wide_row_map(count):
    half = count // 2
    line = np.arange(count + 2 * EDGE)[:, None] - (EDGE - HALO)
    column = np.arange(count)[None, :]
    offset = line - 2 * (column % half)
    return both_taps(offset, column < half)


def in_two(values):
    top = values.astype(jnp.bfloat16)
    return np.stack([top, (values - top.astype(np.float32)).astype(jnp.bfloat16)])


def split(value):
    top = value.astype(jnp.bfloat16)
    return top, (value - top.astype(jnp.float32)).astype(jnp.bfloat16)


def fine_dot(left, right):
    total = jnp.dot(left[0], right[0], preferred_element_type=jnp.float32)
    total = total + jnp.dot(left[1], right[0], preferred_element_type=jnp.float32)
    return total + jnp.dot(left[0], right[1], preferred_element_type=jnp.float32)


def flip(place, bits):
    result = place
    for bit in (1, 2, 4):
        if bits & bit:
            result = result + bit - 2 * bit * (place // bit % 2)
    return result


def iota(shape, dim):
    return lax.broadcasted_iota(jnp.int32, shape, dim)


def whole_kernel(
    n, c, img_far, margin, cells, gains, seen_far, dual_far,
    half_far, edge_far, m1_far, m2_far, rows_far, rows_t_far,
    out, vout,
    img, seen, dual, edge, m1, m2, rows, rows_t, fetched,
    af, bf, hot, marks, cset, gset, dset, vset, vback, rel_of, mod_of,
    send1, recv1, send2, recv2, grid, held, weight,
    padded, halo, coef, sq, sq_in, totals, cpad, spread, bands,
    sa, ra, sb, rb, sh, rh, ss, rs, st, rt, sd, rd, sv, rv,
):
    me = lax.axis_index("slab")
    ch = lax.axis_index("chan")
    count, width = img.shape
    vis = cells.shape[1]
    part, half, side = count // 2, width // 2, n // 2
    tall = count + 2 * EDGE
    pair = 2 * LANES
    block = width // c
    after, before, mate = lax.rem(me + 1, n), lax.rem(me + n - 1, n), n - 1 - me
    upper = me // side
    own = pl.ds(pl.multiple_of(upper * vis, vis), vis)
    other = pl.ds(pl.multiple_of((1 - upper) * vis, vis), vis)
    f32, bf16 = jnp.float32, jnp.bfloat16

    local = [
        (img_far, img), (half_far, af.at[:, :half]), (edge_far, edge),
        (cells, cset.at[:, own]), (gains, gset.at[:, own]), (seen_far, seen), (dual_far, dual),
        (m1_far, m1), (rows_far, rows), (rows_t_far, rows_t), (m2_far, m2),
    ]
    fetches = [
        pltpu.make_async_copy(far, near, fetched.at[i]) for i, (far, near) in enumerate(local)
    ]
    for fetch in fetches:
        fetch.start()

    barrier = pltpu.get_barrier_semaphore()
    for d in range(1, n):
        pl.semaphore_signal(
            barrier, inc=1, device_id={"slab": lax.rem(me + d, n)},
            device_id_type=pl.DeviceIdType.MESH,
        )
    for d in range(1, c):
        pl.semaphore_signal(
            barrier, inc=1, device_id={"chan": lax.rem(ch + d, c)},
            device_id_type=pl.DeviceIdType.MESH,
        )

    def remote(src, dst, s, r, where):
        return pltpu.make_async_remote_copy(
            src_ref=src, dst_ref=dst, send_sem=s, recv_sem=r, device_id=where,
            device_id_type=pl.DeviceIdType.MESH,
        )

    sends = []

    def launch(*args):
        copy = remote(*args)
        copy.start()
        sends.append(copy)
        return copy

    for fetch in fetches[:3]:
        fetch.wait()
    flip_row = (1 - 2 * (iota((count, half), 0) % 2)).astype(f32).astype(bf16)
    for j in range(n):
        here = slice(j * count, (j + 1) * count)
        af[here, half:] = af[here, :half] * flip_row

    flat_b = img[...].astype(bf16)
    spec = lax.dot_general(edge[...], flat_b, crossed, preferred_element_type=f32).astype(bf16)
    for j in range(n):
        k = n - 1 - j
        send1[j, count:, :] = (
            spec[k * TILE : (k + 1) * TILE] if j >= side else jnp.zeros((TILE, count), bf16)
        )

    def spectra(top):
        first = pl.multiple_of(top * half, half)
        spec = lax.dot_general(
            af[pl.ds(first, half), :], flat_b, crossed, preferred_element_type=f32
        ).astype(bf16)
        for j in range(side):
            send1[top * side + j, :count, :] = spec[j * count : (j + 1) * count]

    spectra(1 - upper)
    for fetch in fetches[3:7]:
        fetch.wait()
    dset[:, :, own] = dual[...] - seen[...]

    pl.semaphore_wait(barrier, n + c - 2)
    launch(cset.at[:, own], cset.at[:, own], sv.at[0], rv.at[0], {"slab": mate})
    up = launch(img.at[count - EDGE :], halo.at[0], sh.at[0], rh.at[0], {"slab": after})
    down = launch(img.at[:EDGE], halo.at[1], sh.at[1], rh.at[1], {"slab": before})

    def scatter(bits):
        for d in bits:
            peer = flip(me, d)
            launch(send1.at[peer], recv1.at[me], sa.at[d], ra.at[me], {"slab": peer})

    scatter(range(n - 1, side - 1, -1))
    spectra(upper)
    scatter(range(side - 1, 0, -1))
    launch(gset.at[:, own], gset.at[:, own], sv.at[1], rv.at[1], {"slab": mate})
    launch(dset.at[:, :, own], dset.at[:, :, own], sv.at[2], rv.at[2], {"slab": mate})
    recv1[me] = send1[me]

    def locate(e):
        here = slice(e * vis, (e + 1) * vis)
        spot = cset[:, here]
        column, line = spot // width, spot % width
        if e == 1:
            column = count - column
            line = jnp.where(line == 0, 0, width - line)
        column = column - part * upper
        rel_of[:, here] = jnp.where(column >= part + upper, -1, column)
        mod_of[:, here] = line

    step = 32

    def heat(here):
        line = mod_of[:, here]
        fold = jnp.where(line > half, width - line, jnp.where(line == half, 0, line))

        def body(i, carry):
            hit = jnp.where(iota((step, vis), 0) + i * step == fold, 1.0, 0.0).astype(bf16)
            hot[pl.ds(pl.multiple_of(i * step, step), step), here] = hit
            return carry

        lax.fori_loop(0, half // step, body, 0)

    reach = margin[0]

    def keep(shape, dim):
        line = iota(shape, dim)
        distance = jnp.maximum(jnp.maximum(EDGE - line, line - count - EDGE + 1), 0)
        return jnp.where(distance <= reach, 1.0, 0.0)

    for fetch in fetches[7:]:
        fetch.wait()
    row_fwd = split(rows_t[...] * keep((count, tall), 1))
    row_adj = split(rows[...] * keep((tall, count), 0))

    padded[:, :LANES] = jnp.zeros((tall, LANES), f32)
    padded[:, LANES + width :] = jnp.zeros((tall, LANES), f32)
    padded[EDGE : EDGE + count, LANES : LANES + width] = img[...]
    up.wait_recv()
    down.wait_recv()
    padded[:EDGE, LANES : LANES + width] = jnp.where(me > 0, halo[0], 0.0)
    padded[EDGE + count :, LANES : LANES + width] = jnp.where(me < n - 1, halo[1], 0.0)
    for b in range(width // pair):
        filtered = fine_dot(split(padded[:, b * pair : b * pair + 4 * LANES]), m1)
        piece = fine_dot(row_fwd, split(filtered))
        coef[:, b * pair : (b + 1) * pair] = piece
        sq[:, b * pair : (b + 1) * pair] = (piece * piece).astype(bf16)

    def slot(who):
        return pl.ds(pl.multiple_of(who * block, block), block)

    for d in range(1, c):
        peer = lax.rem(ch + d, c)
        launch(sq.at[:, slot(peer)], sq_in.at[ch], ss.at[d], rs.at[ch], {"chan": peer})

    remote(cset.at[:, other], cset.at[:, other], sv.at[0], rv.at[0], {"slab": mate}).wait_recv()
    locate(0)
    locate(1)
    heat(slice(0, vis))
    heat(slice(vis, 2 * vis))

    flip_lane = (1 - 2 * (iota((part, half), 1) % 2)).astype(f32).astype(bf16)
    nyquist = (1 - 2 * (iota((part, LANES), 0) % 2)).astype(f32) * (1.0 / math.sqrt(width))
    first_lane = iota((part, LANES), 1) == 0
    for j in range(n):
        top = first_column(j, n, count)
        cosine = af[j * count : j * count + part, :half]
        sine = -af[j * count + part : (j + 1) * count, :half]
        mixed = jnp.where(first_lane, nyquist, sine[:, :LANES].astype(f32)).astype(bf16)
        for low, value in ((top, None), (half + top, flip_lane)):
            here = slice(low, low + part)
            bf[here, :half] = cosine if value is None else cosine * value
            rest = sine if value is None else sine * value
            bf[here, half : half + LANES] = (
                mixed if value is None else mixed * value[:, :LANES]
            )
            bf[here, half + LANES :] = rest[:, LANES:]

    for d in range(n - 1, 0, -1):
        src = flip(me, d)
        remote(send1.at[src], recv1.at[src], sa.at[d], ra.at[src], {"slab": src}).wait_recv()
    columns = jnp.concatenate([recv1[j] for j in range(n)], axis=1)
    value = jnp.dot(columns, bf[...], preferred_element_type=f32)
    planes = []
    for lanes in (slice(0, half), slice(half, width)):
        planes.append(
            [value[:part, lanes], value[count : count + EDGE, lanes]]
        )
        planes.append(
            [value[part:count, lanes], value[count + EDGE :, lanes]]
        )
    grid[...] = jnp.concatenate(sum(planes, []), axis=0).astype(bf16)
    deep = part + EDGE

    for d in range(1, c):
        src = lax.rem(ch + d, c)
        remote(sq.at[:, slot(src)], sq_in.at[src], ss.at[d], rs.at[src], {"chan": src}).wait_recv()
    total = sq[:, slot(ch)].astype(f32)
    for d in range(1, c):
        total = total + sq_in[lax.rem(ch + d, c)].astype(f32)
    totals[ch] = total.astype(bf16)
    for d in range(1, c):
        peer = lax.rem(ch + d, c)
        launch(totals.at[ch], totals.at[ch], st.at[d], rt.at[ch], {"chan": peer})

    remote(gset.at[:, other], gset.at[:, other], sv.at[1], rv.at[1], {"slab": mate}).wait_recv()
    remote(dset.at[:, :, other], dset.at[:, :, other], sv.at[2], rv.at[2], {"slab": mate}).wait_recv()

    def factors(line, sign):
        even = jnp.where(line == half, 0.0, 1.0)
        odd = jnp.where(line > half, -1.0, 1.0)
        odd = jnp.where((line == half) | (line == 0), 0.0, odd)
        return even, odd, 1.0 - even

    def spread_out(line, gain, fresh, sign):
        even, odd, last = factors(line, sign)
        real, imag = gain * fresh[0], gain * fresh[1] * sign
        return even * real, even * imag, last * real - odd * imag, odd * real + last * imag

    def visit(i, carry):
        here = pl.ds(pl.multiple_of(i * CHUNK, CHUNK), CHUNK)
        sign = jnp.where(i < vis // CHUNK, 1.0, -1.0)
        found = jnp.dot(grid[...], hot[:, here], preferred_element_type=f32)
        rel = rel_of[:, here]
        match = iota((deep, CHUNK), 0) == rel
        c_re, c_im, s_re, s_im = [
            jnp.sum(
                jnp.where(match, found[k * deep : (k + 1) * deep], 0.0), axis=0, keepdims=True
            )
            for k in range(4)
        ]
        line = mod_of[:, here]
        gain = gset[:, here]
        even, odd, last = factors(line, sign)
        real = even * c_re + odd * s_im + last * s_re
        imag = (even * c_im - odd * s_re + last * s_im) * sign
        fresh = []
        for k, model in enumerate((real, imag)):
            fresh.append((dset[k, :, here] + gain * model) / 2.0)
            vset[k, :, here] = fresh[k]
        near = match[:part]
        for k, mark in enumerate(spread_out(line, gain, fresh, sign)):
            marks[k * part : (k + 1) * part, here] = jnp.where(near, mark, 0.0).astype(bf16)
        return carry

    lax.fori_loop(0, 2 * vis // CHUNK, visit, 0, unroll=2)
    launch(vset.at[:, :, other], vback, sv.at[3], rv.at[3], {"slab": mate})

    def collect(i, carry):
        here = pl.ds(pl.multiple_of(i * pair, pair), pair)
        held[here, :] = lax.dot_general(
            hot[here, :], marks[...], crossed, preferred_element_type=f32
        ).astype(bf16)
        return carry

    lax.fori_loop(0, half // pair, collect, 0)

    coarse, fine = half // 32, 32

    def outer(i, carry):
        here = pl.ds(pl.multiple_of(vis + i * CHUNK, CHUNK), CHUNK)
        line = mod_of[:, here]
        fold = jnp.where(line > half, width - line, jnp.where(line == half, 0, line))
        fresh = [vset[0, :, here], vset[1, :, here]]
        left = jnp.where(iota((coarse, CHUNK), 0) == fold // fine, 1.0, 0.0).astype(bf16)
        match = (iota((fine, CHUNK), 0) == fold % fine) & (rel_of[:, here] == part)
        right = jnp.concatenate(
            [
                jnp.where(match, mark, 0.0).astype(bf16)
                for mark in spread_out(line, gset[:, here], fresh, -1.0)
            ],
            axis=0,
        )
        return carry + lax.dot_general(left, right, crossed, preferred_element_type=f32)

    edges = lax.fori_loop(0, vis // CHUNK, outer, jnp.zeros((coarse, 4 * fine), f32))
    grow = jnp.where(iota((half, coarse), 0) // fine == iota((half, coarse), 1), 1.0, 0.0)
    grown = jnp.dot(grow.astype(bf16), edges.astype(bf16), preferred_element_type=f32)
    lane = iota((half, 4 * fine), 1)
    grown = jnp.where(lane % fine == iota((half, 4 * fine), 0) % fine, grown, 0.0).astype(bf16)
    source, target = iota((4 * fine, LANES), 0) // fine, iota((4 * fine, LANES), 1)
    for k in range(2):
        here = slice(k * half, (k + 1) * half)
        weight[here, :count] = held[:, k * count : (k + 1) * count]
        gather = jnp.where((source - 2 * k == target) & (target < 2), 1.0, 0.0).astype(bf16)
        weight[here, count:] = jnp.dot(grown, gather, preferred_element_type=f32).astype(bf16)

    line, lane = iota((TILE, LANES), 0), iota((TILE, LANES), 1)
    turned = jnp.where(line == EDGE * lane, 1.0, 0.0).astype(bf16)

    def returns(top):
        first = pl.multiple_of(top * half, half)
        back = jnp.dot(
            bf[pl.ds(first, half), :], weight[...], preferred_element_type=f32
        ).astype(bf16)
        tails = lax.dot_general(
            turned, back[:, count:], crossed, preferred_element_type=f32
        ).astype(bf16)
        for j in range(side):
            here = slice(j * count, (j + 1) * count)
            send2[top * side + j, :count, :] = back[here, :count]
            send2[top * side + j, count:, :] = tails[:, here]

    def give(bits):
        for d in bits:
            peer = flip(me, d)
            launch(send2.at[peer], recv2.at[me], sb.at[d], rb.at[me], {"slab": peer})

    returns(1 - upper)
    give(range(n - 1, side - 1, -1))
    returns(upper)
    give(range(side - 1, 0, -1))
    recv2[me] = send2[me]

    for d in range(1, c):
        src = lax.rem(ch + d, c)
        remote(totals.at[src], totals.at[src], st.at[d], rt.at[src], {"chan": src}).wait_recv()
    cpad[:, :pair] = jnp.zeros((count, pair), f32)
    cpad[:, pair + width :] = jnp.zeros((count, pair), f32)
    for j in range(c):
        here = slice(j * block, (j + 1) * block)
        factor = bound_level / jnp.maximum(jnp.sqrt(totals[j].astype(f32)), bound_level)
        cpad[:, pair + j * block : pair + (j + 1) * block] = coef[:, here] * factor
    for b in range(width // pair):
        back = fine_dot(split(cpad[:, b * pair : b * pair + 6 * LANES]), m2)
        spread[:, b * pair : (b + 1) * pair] = fine_dot(row_adj, split(back))
    over = launch(spread.at[count + EDGE :], bands.at[0], sd.at[0], rd.at[0], {"slab": after})
    under = launch(spread.at[:EDGE], bands.at[1], sd.at[1], rd.at[1], {"slab": before})

    remote(vset.at[:, :, other], vback, sv.at[3], rv.at[3], {"slab": mate}).wait_recv()
    mine = rel_of[:, own] >= 0
    for k in range(2):
        vout[k] = jnp.where(mine, vset[k, :, own], vback[k])

    term = None
    for far in range(2):
        for d in range(1 - far, side):
            src = flip(me, d + far * side)
            remote(
                send2.at[src], recv2.at[src], sb.at[d + far * side], rb.at[src], {"slab": src}
            ).wait_recv()
        first = (upper + far) % 2
        row = jnp.concatenate([recv2[first * side + j, :count, :] for j in range(side)], axis=1)
        here = pl.ds(pl.multiple_of(first * half, half), half)
        more = jnp.dot(row, af[here, :], preferred_element_type=f32)
        term = more if term is None else term + more
    tails = jnp.concatenate([recv2[n - 1 - k, count:, :] for k in range(side)], axis=0)
    term = term + lax.dot_general(tails, edge[...], leading, preferred_element_type=f32)
    over.wait_recv()
    under.wait_recv()
    wave_first = spread[EDGE : 2 * EDGE, :] + jnp.where(me > 0, bands[0], 0.0)
    wave_last = spread[count : count + EDGE, :] + jnp.where(me < n - 1, bands[1], 0.0)
    wave = jnp.concatenate(
        [wave_first, spread[2 * EDGE : count, :], wave_last], axis=0
    )
    out[...] = jnp.maximum(img[...] - tau_step * (term + wave), 0.0)

    for copy in sends:
        copy.wait_send()


def local_kernel(n, c, image, margin, cells, weights, observed, dual_start):
    count, width = image.shape[1], image.shape[2]
    vis = cells.shape[1]
    tall = count + 2 * EDGE
    part, half = count // 2, width // 2
    half_t, f32 = jnp.bfloat16, jnp.float32
    V = pltpu.VMEM
    dma = pltpu.SemaphoreType.DMA
    row_map = wide_row_map(count)
    vm = pl.BlockSpec(memory_space=pltpu.VMEM)
    anywhere = pl.BlockSpec(memory_space=pl.ANY)
    fresh, dual = pl.pallas_call(
        functools.partial(whole_kernel, n, c),
        out_shape=(
            jax.ShapeDtypeStruct((count, width), f32),
            jax.ShapeDtypeStruct((2, 1, vis), f32),
        ),
        in_specs=[anywhere, pl.BlockSpec(memory_space=pltpu.SMEM)] + [anywhere] * 10,
        out_specs=(vm, vm),
        scratch_shapes=[
            V((count, width), f32),
            V((2, 1, vis), f32),
            V((2, 1, vis), f32),
            V((n // 2 * TILE, width), half_t),
            V((2, 4 * LANES, 2 * LANES), half_t),
            V((2, 6 * LANES, 2 * LANES), half_t),
            V((tall, count), f32),
            V((count, tall), f32),
            dma((11,)),
            V((width, width), half_t),
            V((width, width), half_t),
            V((half, 2 * vis), half_t),
            V((2 * count, 2 * vis), half_t),
            V((1, 2 * vis), jnp.int32),
            V((1, 2 * vis), f32),
            V((2, 1, 2 * vis), f32),
            V((2, 1, 2 * vis), f32),
            V((2, 1, vis), f32),
            V((1, 2 * vis), jnp.int32),
            V((1, 2 * vis), jnp.int32),
            V((n, count + TILE, count), half_t),
            V((n, count + TILE, count), half_t),
            V((n, count + TILE, count), half_t),
            V((n, count + TILE, count), half_t),
            V((4 * (part + EDGE), half), half_t),
            V((half, 2 * count), half_t),
            V((width, 2 * count), half_t),
            V((tall, width + 2 * LANES), f32),
            V((2, EDGE, width), f32),
            V((count, width), f32),
            V((count, width), half_t),
            V((c, count, width // c), half_t),
            V((c, count, width // c), half_t),
            V((count, width + 4 * LANES), f32),
            V((tall, width), f32),
            V((2, EDGE, width), f32),
            dma((n,)), dma((n,)), dma((n,)), dma((n,)), dma((2,)), dma((2,)),
            dma((c,)), dma((c,)), dma((c,)), dma((c,)), dma((2,)), dma((2,)),
            dma((4,)), dma((4,)),
        ],
        compiler_params=pltpu.CompilerParams(
            collective_id=0, has_side_effects=True, vmem_limit_bytes=60 * 1024 * 1024
        ),
    )(
        image[0], margin, cells, weights, observed, dual_start,
        owner_table(n, count, width), edge_table(n, count, width),
        in_two(analysis_map()), in_two(synthesis_map()),
        row_map, np.ascontiguousarray(row_map.T),
    )
    return (fresh[None], dual)


def solution(mesh):
    n, c = mesh.shape["slab"], mesh.shape["chan"]

    def local(image, *rest):
        count, width = image.shape[1], image.shape[2]
        fits = n == 8 and count == LANES and width == n * count and width % (c * LANES) == 0
        if fits and rest[1].shape[1] % CHUNK == 0:
            return local_kernel(n, c, image, *rest)
        return local_plain(image, *rest)

    in_specs = (
        P("chan", "slab", None),
        P("slab"),
        P("chan", "slab"),
        P("chan", "slab"),
        P(None, "chan", "slab"),
        P(None, "chan", "slab"),
    )
    out_specs = (P("chan", "slab", None), P(None, "chan", "slab"))
    return jax.shard_map(local, mesh=mesh, in_specs=in_specs, out_specs=out_specs, check_vma=False)
```

```python
import functools
import math

import jax
import jax.numpy as jnp
import numpy as np
from jax import lax
from jax.experimental import pallas as pl
from jax.experimental.pallas import tpu as pltpu
from jax.sharding import PartitionSpec as P

N = 1024
HALO = 3


low_taps = (
    -0.010597401784997278,
    0.032883011666982945,
    0.030841381835986965,
    -0.18703481171888114,
    -0.02798376941698385,
    0.6308807679295904,
    0.7148465705525415,
    0.23037781330885523,
)
high_taps = (
    -0.23037781330885523,
    0.7148465705525415,
    -0.6308807679295904,
    -0.02798376941698385,
    0.18703481171888114,
    0.030841381835986965,
    -0.032883011666982945,
    -0.010597401784997278,
)
tau_step = 0.5
bound_level = 3.0
leading = (((0,), (0,)), ((), ()))


def with_halo(block, sides, width):
    for axis, dim in sides:
        count = lax.axis_size(axis)
        forward = [(i, i + 1) for i in range(count - 1)]
        backward = [(target, source) for source, target in forward]
        low = lax.ppermute(
            lax.slice_in_dim(block, block.shape[dim] - width, None, axis=dim), axis, forward
        )
        high = lax.ppermute(lax.slice_in_dim(block, 0, width, axis=dim), axis, backward)
        block = jnp.concatenate([low, block, high], axis=dim)
    return block


def tap_value(offset, taps):
    total = jnp.zeros(offset.shape, jnp.float32)
    for position in range(8):
        total = total + jnp.where(offset == position, taps[position], 0.0).astype(jnp.float32)
    return total


def fourier_tables(length):
    index = jnp.arange(length, dtype=jnp.int32)
    product = index[:, None] * index[None, :] % length
    angle = product.astype(jnp.float32) * (2.0 * math.pi / length)
    scale = 1.0 / math.sqrt(length)
    return (
        (jnp.cos(angle) * scale).astype(jnp.bfloat16),
        (jnp.sin(angle) * scale).astype(jnp.bfloat16),
    )


def row_matrix(count):
    half = count // 2
    line = jnp.arange(count + 2 * HALO, dtype=jnp.int32)[:, None]
    column = jnp.arange(count, dtype=jnp.int32)[None, :]
    offset = line - 2 * (column % half)
    return jnp.where(column < half, tap_value(offset, low_taps), tap_value(offset, high_taps))


def facet_mask(count, width):
    line = jnp.arange(count + 2 * HALO, dtype=jnp.int32)
    distance = jnp.maximum(jnp.maximum(HALO - line, line - count - HALO + 1), 0)
    return (distance[None, :] <= width[:, None]).astype(jnp.float32)


def column_forward(values):
    width = values.shape[1]
    half = width // 2
    padded = jnp.pad(values, ((0, 0), (HALO, 8)))
    even_cells = padded[:, 0::2]
    odd_cells = padded[:, 1::2]
    low_part = jnp.zeros((values.shape[0], half), jnp.float32)
    high_part = jnp.zeros((values.shape[0], half), jnp.float32)
    for position in range(8):
        source = even_cells if position % 2 == 0 else odd_cells
        piece = source[:, position // 2 : position // 2 + half]
        low_part = low_part + low_taps[position] * piece
        high_part = high_part + high_taps[position] * piece
    return jnp.concatenate([low_part, high_part], axis=1)


def column_adjoint(coefs):
    width = coefs.shape[1]
    half = width // 2
    low_part = coefs[:, :half]
    high_part = coefs[:, half:]
    even_sums = jnp.zeros((coefs.shape[0], half + 4), jnp.float32)
    odd_sums = jnp.zeros((coefs.shape[0], half + 4), jnp.float32)
    for position in range(8):
        term = low_taps[position] * low_part + high_taps[position] * high_part
        placed = jnp.pad(term, ((0, 0), (position // 2, 4 - position // 2)))
        if position % 2 == 0:
            even_sums = even_sums + placed
        else:
            odd_sums = odd_sums + placed
    joined = jnp.stack([even_sums, odd_sums], axis=2).reshape(coefs.shape[0], width + 8)
    return joined[:, HALO : HALO + width]


def data_part(lifted, dual, seen, places, gains, cos_table, sin_table):
    flat_b = lifted.astype(jnp.bfloat16)
    spectra = jnp.stack(
        [
            jnp.dot(flat_b, cos_table, preferred_element_type=jnp.float32),
            -jnp.dot(flat_b, sin_table, preferred_element_type=jnp.float32),
        ]
    ).astype(jnp.bfloat16)
    columns = lax.all_to_all(spectra, "slab", split_axis=2, concat_axis=1, tiled=True)
    grid_real = lax.dot_general(
        columns[0], cos_table, leading, preferred_element_type=jnp.float32
    ) + lax.dot_general(columns[1], sin_table, leading, preferred_element_type=jnp.float32)
    grid_imag = lax.dot_general(
        columns[1], cos_table, leading, preferred_element_type=jnp.float32
    ) - lax.dot_general(columns[0], sin_table, leading, preferred_element_type=jnp.float32)
    model = jnp.stack(
        [gains * grid_real.reshape(-1)[places], gains * grid_imag.reshape(-1)[places]]
    )
    fresh_dual = (dual + (model - seen)) / 2.0
    weighted = gains[None, :] * fresh_dual
    cell_count = grid_real.size
    hold_real = (
        jnp.zeros((cell_count,), jnp.float32)
        .at[places]
        .add(weighted[0])
        .reshape(grid_real.shape)
        .astype(jnp.bfloat16)
    )
    hold_imag = (
        jnp.zeros((cell_count,), jnp.float32)
        .at[places]
        .add(weighted[1])
        .reshape(grid_real.shape)
        .astype(jnp.bfloat16)
    )
    backward = jnp.stack(
        [
            jnp.dot(hold_real, cos_table, preferred_element_type=jnp.float32)
            - jnp.dot(hold_imag, sin_table, preferred_element_type=jnp.float32),
            jnp.dot(hold_real, sin_table, preferred_element_type=jnp.float32)
            + jnp.dot(hold_imag, cos_table, preferred_element_type=jnp.float32),
        ]
    ).astype(jnp.bfloat16)
    returned = lax.all_to_all(backward, "slab", split_axis=2, concat_axis=1, tiled=True)
    data_term = lax.dot_general(
        returned[0], cos_table, leading, preferred_element_type=jnp.float32
    ) - lax.dot_general(returned[1], sin_table, leading, preferred_element_type=jnp.float32)
    return (data_term, fresh_dual)


def wave_part(lifted, row_map, mask):
    highest = lax.Precision.HIGHEST
    count = lifted.shape[0]
    extended = with_halo(lifted, (("slab", 0),), HALO) * mask
    filtered = column_forward(extended)
    coef = lax.dot_general(
        row_map, filtered, leading, precision=highest, preferred_element_type=jnp.float32
    )
    squares = coef * coef
    share = lax.psum_scatter(
        squares.astype(jnp.bfloat16), "chan", scatter_dimension=1, tiled=True
    ).astype(jnp.float32)
    partial_factor = bound_level / jnp.maximum(jnp.sqrt(share), bound_level)
    factor = lax.all_gather(partial_factor, "chan", axis=1, tiled=True)
    fresh_dual = coef * factor
    back = column_adjoint(fresh_dual)
    spread = jnp.dot(row_map, back, precision=highest, preferred_element_type=jnp.float32) * mask
    bands = jnp.concatenate([spread[:HALO], spread[count + HALO :]], axis=0)
    arrived = with_halo(bands, (("slab", 0),), HALO)
    inner = spread[HALO : count + HALO]
    inner = inner.at[:HALO].add(arrived[:HALO])
    inner = inner.at[count - HALO :].add(arrived[3 * HALO :])
    return (inner, fresh_dual)


def local_plain(image, margin, cells, weights, observed, dual_start):
    count = image.shape[1]
    cos_table, sin_table = fourier_tables(N)
    row_map = row_matrix(count)
    mask = facet_mask(count, margin)[0][:, None]
    places = cells[0]
    gains = weights[0]
    seen = observed[:, 0, :]
    dual = dual_start[:, 0, :]
    estimate = image[0]
    data_term, dual = data_part(estimate, dual, seen, places, gains, cos_table, sin_table)
    wave_term, wave_dual = wave_part(estimate, row_map, mask)
    fresh = jnp.maximum(estimate - tau_step * (data_term + wave_term), 0.0)
    return (fresh[None], dual[:, None, :])


LANES = 128
EDGE = 8
CHUNK = 512
TILE = 16
highest = lax.Precision.HIGHEST
crossed = (((1,), (1,)), ((), ()))


def pick(offset, taps):
    inside = (offset >= 0) & (offset < 8)
    return np.where(inside, np.asarray(taps, np.float64)[np.clip(offset, 0, 7)], 0.0)


def both_taps(offset, is_low):
    return np.where(is_low, pick(offset, low_taps), pick(offset, high_taps)).astype(np.float32)


def wave_rows(lines, length, span):
    angle = lines[:, None] * np.arange(span)[None, :] % length * (2.0 * np.pi / length)
    scale = 1.0 / np.sqrt(length)
    return np.cos(angle) * scale, -np.sin(angle) * scale


def first_column(owner, n, count):
    return count * owner if owner < n // 2 else count * (n - 1 - owner) + count // 2


def owner_table(n, count, width):
    blocks = []
    few = count // 4
    for h in range(2):
        for owner in range(n):
            lines = first_column(owner, n, count) + h * few + np.arange(few)
            blocks.extend(wave_rows(lines, width, width // 2))
    return np.concatenate(blocks).astype(np.float32).astype(jnp.bfloat16)


def edge_table(n, count, width):
    table = np.zeros((n // 2, TILE, width), np.float32)
    real, imag = wave_rows(count * (1 + np.arange(n // 2)), width, width)
    table[:, 0], table[:, TILE // 2] = real, imag
    return table.reshape(-1, width).astype(jnp.bfloat16)


def analysis_map():
    line = np.arange(4 * LANES)[:, None]
    column = np.arange(2 * LANES)[None, :]
    offset = line - (LANES - HALO) - 2 * (column % LANES)
    return both_taps(offset, column < LANES)


def synthesis_map():
    line = np.arange(6 * LANES)[:, None]
    column = np.arange(2 * LANES)[None, :]
    block = line // (2 * LANES) - 1
    offset = column - 2 * LANES * block - 2 * (line % LANES) + HALO
    return both_taps(offset, line % (2 * LANES) < LANES)


def wide_row_map(count):
    half = count // 2
    line = np.arange(count + 2 * EDGE)[:, None] - (EDGE - HALO)
    column = np.arange(count)[None, :]
    offset = line - 2 * (column % half)
    return both_taps(offset, column < half)


def in_two(values):
    top = values.astype(jnp.bfloat16)
    return np.stack([top, (values - top.astype(np.float32)).astype(jnp.bfloat16)])


def split(value):
    top = value.astype(jnp.bfloat16)
    return top, (value - top.astype(jnp.float32)).astype(jnp.bfloat16)


def fine_dot(left, right):
    total = jnp.dot(left[0], right[0], preferred_element_type=jnp.float32)
    total = total + jnp.dot(left[1], right[0], preferred_element_type=jnp.float32)
    return total + jnp.dot(left[0], right[1], preferred_element_type=jnp.float32)


def flip(place, bits):
    result = place
    for bit in (1, 2, 4):
        if bits & bit:
            result = result + bit - 2 * bit * (place // bit % 2)
    return result


def iota(shape, dim):
    return lax.broadcasted_iota(jnp.int32, shape, dim)


def whole_kernel(
    n, c, img_far, margin, cells, gains, seen_far, dual_far,
    half_far, edge_far, m1_far, m2_far, rows_far, rows_t_far,
    out, vout,
    img, seen, dual, edge, m1, m2, rows, rows_t, fetched,
    af, bf, hot, marks, cset, gset, dset, vset, vback, rel_of, mod_of, fold_of, warm,
    send1, recv1, send2, recv2, send3, recv3, grid, weight, extra,
    padded, halo, coef, sq, sq_in, totals, cpad, spread, bands,
    sa, ra, sb, rb, sh, rh, ss, rs, st, rt, sd, rd, sv, rv, sw, rw,
):
    me = lax.axis_index("slab")
    ch = lax.axis_index("chan")
    count, width = img.shape
    vis = cells.shape[1]
    part, half, side, few = count // 2, width // 2, n // 2, count // 4
    tall = count + 2 * EDGE
    pair = 2 * LANES
    block = width // c
    after, before, mate = lax.rem(me + 1, n), lax.rem(me + n - 1, n), n - 1 - me
    upper = me // side
    own = pl.ds(pl.multiple_of(upper * vis, vis), vis)
    other = pl.ds(pl.multiple_of((1 - upper) * vis, vis), vis)
    f32, bf16 = jnp.float32, jnp.bfloat16

    local = [
        (img_far, img), (half_far, af.at[:, :half]), (edge_far, edge),
        (cells, cset.at[:, own]), (gains, gset.at[:, own]), (seen_far, seen), (dual_far, dual),
        (m1_far, m1), (rows_far, rows), (rows_t_far, rows_t), (m2_far, m2),
    ]
    fetches = [
        pltpu.make_async_copy(far, near, fetched.at[i]) for i, (far, near) in enumerate(local)
    ]
    for fetch in fetches:
        fetch.start()

    barrier = pltpu.get_barrier_semaphore()
    for d in range(1, n):
        pl.semaphore_signal(
            barrier, inc=1, device_id={"slab": lax.rem(me + d, n)},
            device_id_type=pl.DeviceIdType.MESH,
        )
    for d in range(1, c):
        pl.semaphore_signal(
            barrier, inc=1, device_id={"chan": lax.rem(ch + d, c)},
            device_id_type=pl.DeviceIdType.MESH,
        )

    def remote(src, dst, s, r, where):
        return pltpu.make_async_remote_copy(
            src_ref=src, dst_ref=dst, send_sem=s, recv_sem=r, device_id=where,
            device_id_type=pl.DeviceIdType.MESH,
        )

    sends = []

    def launch(*args):
        copy = remote(*args)
        copy.start()
        sends.append(copy)
        return copy

    for fetch in fetches[:3]:
        fetch.wait()
    flip_row = (1 - 2 * (iota((count, half), 0) % 2)).astype(f32).astype(bf16)
    for j in range(n):
        here = slice(j * count, (j + 1) * count)
        af[here, half:] = af[here, :half] * flip_row

    flat_b = img[...].astype(bf16)
    send1[0, :, part:, :] = jnp.zeros((n, TILE, count), bf16)
    spec = lax.dot_general(edge[...], flat_b, crossed, preferred_element_type=f32).astype(bf16)
    for j in range(n):
        k = n - 1 - j
        send1[1, j, part:, :] = (
            spec[k * TILE : (k + 1) * TILE] if j >= side else jnp.zeros((TILE, count), bf16)
        )

    def spectra(h):
        spec = lax.dot_general(
            af[h * half : (h + 1) * half, :], flat_b, crossed, preferred_element_type=f32
        ).astype(bf16)
        for j in range(n):
            send1[h, j, :part, :] = spec[j * part : (j + 1) * part]

    def outward(h, src, peer, d, home):
        rows = part if h == 0 else part + TILE
        return remote(
            send1.at[h, src, :rows], recv1.at[h, home, :rows], sa.at[h, d], ra.at[h, home],
            {"slab": peer},
        )

    def scatter(h):
        for d in range(n - 1, 0, -1):
            peer = flip(me, d)
            copy = outward(h, peer, peer, d, me)
            copy.start()
            sends.append(copy)
        recv1[h, me] = send1[h, me]

    fetches[3].wait()
    pl.semaphore_wait(barrier, n + c - 2)
    launch(cset.at[:, own], cset.at[:, own], sv.at[0], rv.at[0], {"slab": mate})
    spectra(0)
    scatter(0)
    up = launch(img.at[count - EDGE :], halo.at[0], sh.at[0], rh.at[0], {"slab": after})
    down = launch(img.at[:EDGE], halo.at[1], sh.at[1], rh.at[1], {"slab": before})
    spectra(1)
    scatter(1)
    for fetch in fetches[4:7]:
        fetch.wait()
    dset[:, :, own] = dual[...] - seen[...]
    launch(gset.at[:, own], gset.at[:, own], sv.at[1], rv.at[1], {"slab": mate})
    launch(dset.at[:, :, own], dset.at[:, :, own], sv.at[2], rv.at[2], {"slab": mate})

    def locate(here, sign):
        spot = cset[:, here]
        column, line = spot // width, spot % width
        column = jnp.where(sign > 0, column, count - column) - part * upper
        line = jnp.where((sign > 0) | (line == 0), line, width - line)
        rel_of[:, here] = jnp.where(column >= part + upper, -1, column)
        mod_of[:, here] = line
        fold = jnp.where(line > half, width - line, jnp.where(line == half, 0, line))
        fold_of[:, here] = fold

    step = 32

    def heat(here):
        fold = fold_of[:, here]

        def body(i, carry):
            hit = jnp.where(iota((step, vis), 0) + i * step == fold, 1.0, 0.0).astype(bf16)
            hot[pl.ds(pl.multiple_of(i * step, step), step), here] = hit
            return carry

        lax.fori_loop(0, half // step, body, 0)
        fold = fold % (half // 2)

        def again(i, carry):
            hit = jnp.where(iota((step, vis), 0) + i * step == fold, 1.0, 0.0).astype(bf16)
            warm[pl.ds(pl.multiple_of(i * step, step), step), here] = hit
            return carry

        lax.fori_loop(0, half // 2 // step, again, 0)

    locate(own, 1 - 2 * upper)
    heat(own)

    reach = margin[0]

    def keep(shape, dim):
        line = iota(shape, dim)
        distance = jnp.maximum(jnp.maximum(EDGE - line, line - count - EDGE + 1), 0)
        return jnp.where(distance <= reach, 1.0, 0.0)

    for fetch in fetches[7:]:
        fetch.wait()
    row_fwd = split(rows_t[...] * keep((count, tall), 1))
    row_adj = split(rows[...] * keep((tall, count), 0))

    flip_lane = (1 - 2 * (iota((few, half), 1) % 2)).astype(f32).astype(bf16)
    nyquist = (1 - 2 * (iota((few, LANES), 0) % 2)).astype(f32) * (1.0 / math.sqrt(width))
    first_lane = iota((few, LANES), 1) == 0
    for j in range(2 * n):
        top = first_column(j % n, n, count) + j // n * few
        cosine = af[j * part : j * part + few, :half]
        sine = -af[j * part + few : (j + 1) * part, :half]
        mixed = jnp.where(first_lane, nyquist, sine[:, :LANES].astype(f32)).astype(bf16)
        for low, value in ((top, None), (half + top, flip_lane)):
            here = slice(low, low + few)
            bf[here, :half] = cosine if value is None else cosine * value
            rest = sine if value is None else sine * value
            bf[here, half : half + LANES] = (
                mixed if value is None else mixed * value[:, :LANES]
            )
            bf[here, half + LANES :] = rest[:, LANES:]

    padded[:, :LANES] = jnp.zeros((tall, LANES), f32)
    padded[:, LANES + width :] = jnp.zeros((tall, LANES), f32)
    padded[EDGE : EDGE + count, LANES : LANES + width] = img[...]
    up.wait_recv()
    down.wait_recv()
    padded[:EDGE, LANES : LANES + width] = jnp.where(me > 0, halo[0], 0.0)
    padded[EDGE + count :, LANES : LANES + width] = jnp.where(me < n - 1, halo[1], 0.0)
    for b in range(width // pair):
        filtered = fine_dot(split(padded[:, b * pair : b * pair + 4 * LANES]), m1)
        piece = fine_dot(row_fwd, split(filtered))
        coef[:, b * pair : (b + 1) * pair] = piece
        sq[:, b * pair : (b + 1) * pair] = (piece * piece).astype(bf16)

    def slot(who):
        return pl.ds(pl.multiple_of(who * block, block), block)

    for d in range(1, c):
        peer = lax.rem(ch + d, c)
        launch(sq.at[:, slot(peer)], sq_in.at[ch], ss.at[d], rs.at[ch], {"chan": peer})

    remote(cset.at[:, other], cset.at[:, other], sv.at[0], rv.at[0], {"slab": mate}).wait_recv()
    locate(other, 2 * upper - 1)
    heat(other)

    def arrive(h):
        for d in range(n - 1, 0, -1):
            src = flip(me, d)
            outward(h, src, src, d, src).wait_recv()
        rows = part if h == 0 else part + TILE
        columns = jnp.concatenate([recv1[h, j, :rows] for j in range(n)], axis=1)
        value = jnp.dot(columns, bf[...], preferred_element_type=f32)
        planes = []
        for lanes in (slice(0, half), slice(half, width)):
            for k in range(2):
                planes.append(value[k * few : (k + 1) * few, lanes])
                if h == 1:
                    planes.append(value[part + k * EDGE : part + (k + 1) * EDGE, lanes])
        rows = sum(plane.shape[0] for plane in planes)
        grid[:rows] = jnp.concatenate(planes, axis=0).astype(bf16)

    def factors(line, sign):
        even = jnp.where(line == half, 0.0, 1.0)
        odd = jnp.where(line > half, -1.0, 1.0)
        odd = jnp.where((line == half) | (line == 0), 0.0, odd)
        return even, odd, 1.0 - even

    def spread_out(line, gain, fresh, sign):
        even, odd, last = factors(line, sign)
        real, imag = gain * fresh[0], gain * fresh[1] * sign
        return even * real, even * imag, last * real - odd * imag, odd * real + last * imag

    def visit(h, base, sign, i, carry):
        here = pl.ds(pl.multiple_of(base * vis + i * CHUNK, CHUNK), CHUNK)
        deep = few + h * EDGE
        found = jnp.dot(grid[: 4 * deep], hot[:, here], preferred_element_type=f32)
        rel = rel_of[:, here] - h * few
        match = iota((deep, CHUNK), 0) == rel
        c_re, c_im, s_re, s_im = [
            jnp.sum(
                jnp.where(match, found[k * deep : (k + 1) * deep], 0.0), axis=0, keepdims=True
            )
            for k in range(4)
        ]
        line = mod_of[:, here]
        gain = gset[:, here]
        even, odd, last = factors(line, sign)
        real = even * c_re + odd * s_im + last * s_re
        imag = (even * c_im - odd * s_re + last * s_im) * sign
        fresh = []
        for k, model in enumerate((real, imag)):
            fresh.append((dset[k, :, here] + gain * model) / 2.0)
            vset[k, :, here] = (
                fresh[k] if h == 0 else jnp.where(rel >= 0, fresh[k], vset[k, :, here])
            )
        late = fold_of[:, here] >= half // 2
        values = spread_out(line, gain, fresh, sign)
        for v in range(2):
            near = iota((few, CHUNK), 0) == jnp.where(late == (v == 1), rel, -1)
            for k, mark in enumerate(values):
                low = (v * 4 + k) * few
                marks[low : low + few, here] = jnp.where(near, mark, 0.0).astype(bf16)
        return carry

    facing = (1 - 2 * upper).astype(f32)
    span = 2 * vis // 4

    def collect(i, carry):
        here = pl.ds(pl.multiple_of(i * span, span), span)
        return carry + lax.dot_general(
            warm[:, here], marks[:, here], crossed, preferred_element_type=f32
        )

    flat = jnp.where(iota((part, LANES), 0) == iota((part, LANES), 1), 1.0, 0.0).astype(bf16)

    def returns(h, top):
        first = pl.multiple_of(top * half, half)
        back = jnp.dot(
            bf[pl.ds(first, half), :], weight[...], preferred_element_type=f32
        ).astype(bf16)
        turned = lax.dot_general(
            flat, back, crossed, preferred_element_type=f32
        ).astype(bf16)
        for j in range(side):
            send2[h, top * side + j] = turned[:, j * count : (j + 1) * count]

    def inward(h, src, peer, d, home):
        return remote(
            send2.at[h, src], recv2.at[h, home], sb.at[h, d], rb.at[h, home], {"slab": peer}
        )

    def give(h, bits):
        for d in bits:
            peer = flip(me, d)
            copy = inward(h, peer, peer, d, me)
            copy.start()
            sends.append(copy)

    for h in range(2):
        arrive(h)
        if h == 0:
            here_first = functools.partial(visit, h, upper, facing)
            lax.fori_loop(0, vis // CHUNK, here_first, 0, unroll=2)
            remote(
                gset.at[:, other], gset.at[:, other], sv.at[1], rv.at[1], {"slab": mate}
            ).wait_recv()
            remote(
                dset.at[:, :, other], dset.at[:, :, other], sv.at[2], rv.at[2], {"slab": mate}
            ).wait_recv()
        else:
            here_first = functools.partial(visit, h, upper, facing)
            lax.fori_loop(0, vis // CHUNK, here_first, 0, unroll=2)
        there = functools.partial(visit, h, 1 - upper, -facing)
        lax.fori_loop(0, vis // CHUNK, there, 0, unroll=2)
        if h == 1:
            launch(vset.at[:, :, other], vback, sv.at[3], rv.at[3], {"slab": mate})
        held = lax.fori_loop(0, 4, collect, jnp.zeros((half // 2, 2 * count), f32))
        for v in range(2):
            low = v * (half // 2)
            mine = held[:, v * count : (v + 1) * count]
            weight[low : low + half // 2, :] = mine.astype(bf16)
            mine = jnp.concatenate([mine[:, part:], mine[:, :part]], axis=1)
            weight[half + low : half + low + half // 2, :] = mine.astype(bf16)
        returns(h, 1 - upper)
        give(h, range(n - 1, side - 1, -1))
        returns(h, upper)
        give(h, range(side - 1, 0, -1))
        recv2[h, me] = send2[h, me]
        if h == 0:
            for d in range(1, c):
                src = lax.rem(ch + d, c)
                remote(sq.at[:, slot(src)], sq_in.at[src], ss.at[d], rs.at[src], {"chan": src}).wait_recv()
            total = sq[:, slot(ch)].astype(f32)
            for d in range(1, c):
                total = total + sq_in[lax.rem(ch + d, c)].astype(f32)
            totals[ch] = total.astype(bf16)
            for d in range(1, c):
                peer = lax.rem(ch + d, c)
                launch(totals.at[ch], totals.at[ch], st.at[d], rt.at[ch], {"chan": peer})

    coarse, fine = half // 32, 32

    def outer(i, carry):
        here = pl.ds(pl.multiple_of(vis + i * CHUNK, CHUNK), CHUNK)
        line = mod_of[:, here]
        fold = jnp.where(line > half, width - line, jnp.where(line == half, 0, line))
        fresh = [vset[0, :, here], vset[1, :, here]]
        left = jnp.where(iota((coarse, CHUNK), 0) == fold // fine, 1.0, 0.0).astype(bf16)
        match = (iota((fine, CHUNK), 0) == fold % fine) & (rel_of[:, here] == part)
        right = jnp.concatenate(
            [
                jnp.where(match, mark, 0.0).astype(bf16)
                for mark in spread_out(line, gset[:, here], fresh, -1.0)
            ],
            axis=0,
        )
        return carry + lax.dot_general(left, right, crossed, preferred_element_type=f32)

    edges = lax.fori_loop(0, vis // CHUNK, outer, jnp.zeros((coarse, 4 * fine), f32))
    grow = jnp.where(iota((half, coarse), 0) // fine == iota((half, coarse), 1), 1.0, 0.0)
    grown = jnp.dot(grow.astype(bf16), edges.astype(bf16), preferred_element_type=f32)
    lane = iota((half, 4 * fine), 1)
    grown = jnp.where(lane % fine == iota((half, 4 * fine), 0) % fine, grown, 0.0).astype(bf16)
    source, target = iota((4 * fine, LANES), 0) // fine, iota((4 * fine, LANES), 1)
    for k in range(2):
        here = slice(k * half, (k + 1) * half)
        gather = jnp.where((source - 2 * k == target) & (target < 2), 1.0, 0.0).astype(bf16)
        extra[here, :] = jnp.dot(grown, gather, preferred_element_type=f32).astype(bf16)

    line, lane = iota((TILE, LANES), 0), iota((TILE, LANES), 1)
    turned = jnp.where(line == EDGE * lane, 1.0, 0.0).astype(bf16)

    back = jnp.dot(bf[...], extra[...], preferred_element_type=f32).astype(bf16)
    tails = lax.dot_general(turned, back, crossed, preferred_element_type=f32).astype(bf16)
    for j in range(n):
        send3[j] = tails[:, j * count : (j + 1) * count]
    for d in range(n - 1, 0, -1):
        peer = flip(me, d)
        launch(send3.at[peer], recv3.at[me], sw.at[d], rw.at[me], {"slab": peer})
    recv3[me] = send3[me]

    for d in range(1, c):
        src = lax.rem(ch + d, c)
        remote(totals.at[src], totals.at[src], st.at[d], rt.at[src], {"chan": src}).wait_recv()
    cpad[:, :pair] = jnp.zeros((count, pair), f32)
    cpad[:, pair + width :] = jnp.zeros((count, pair), f32)
    for j in range(c):
        here = slice(j * block, (j + 1) * block)
        factor = bound_level / jnp.maximum(jnp.sqrt(totals[j].astype(f32)), bound_level)
        cpad[:, pair + j * block : pair + (j + 1) * block] = coef[:, here] * factor
    for b in range(width // pair):
        back = fine_dot(split(cpad[:, b * pair : b * pair + 6 * LANES]), m2)
        spread[:, b * pair : (b + 1) * pair] = fine_dot(row_adj, split(back))
    over = launch(spread.at[count + EDGE :], bands.at[0], sd.at[0], rd.at[0], {"slab": after})
    under = launch(spread.at[:EDGE], bands.at[1], sd.at[1], rd.at[1], {"slab": before})

    remote(vset.at[:, :, other], vback, sv.at[3], rv.at[3], {"slab": mate}).wait_recv()
    mine = rel_of[:, own] >= 0
    for k in range(2):
        vout[k] = jnp.where(mine, vset[k, :, own], vback[k])

    term = None
    for h in range(2):
        for d in range(n - 1, 0, -1):
            src = flip(me, d)
            inward(h, src, src, d, src).wait_recv()
        row = jnp.concatenate([recv2[h, j] for j in range(n)], axis=0)
        more = lax.dot_general(
            row, af[h * half : (h + 1) * half, :], leading, preferred_element_type=f32
        )
        term = more if term is None else term + more
    for d in range(n - 1, 0, -1):
        src = flip(me, d)
        remote(send3.at[src], recv3.at[src], sw.at[d], rw.at[src], {"slab": src}).wait_recv()
    tails = jnp.concatenate([recv3[n - 1 - k] for k in range(side)], axis=0)
    term = term + lax.dot_general(tails, edge[...], leading, preferred_element_type=f32)
    over.wait_recv()
    under.wait_recv()
    wave_first = spread[EDGE : 2 * EDGE, :] + jnp.where(me > 0, bands[0], 0.0)
    wave_last = spread[count : count + EDGE, :] + jnp.where(me < n - 1, bands[1], 0.0)
    wave = jnp.concatenate(
        [wave_first, spread[2 * EDGE : count, :], wave_last], axis=0
    )
    out[...] = jnp.maximum(img[...] - tau_step * (term + wave), 0.0)

    for copy in sends:
        copy.wait_send()


def local_kernel(n, c, image, margin, cells, weights, observed, dual_start):
    count, width = image.shape[1], image.shape[2]
    vis = cells.shape[1]
    tall = count + 2 * EDGE
    part, half = count // 2, width // 2
    half_t, f32 = jnp.bfloat16, jnp.float32
    V = pltpu.VMEM
    dma = pltpu.SemaphoreType.DMA
    row_map = wide_row_map(count)
    vm = pl.BlockSpec(memory_space=pltpu.VMEM)
    anywhere = pl.BlockSpec(memory_space=pl.ANY)
    fresh, dual = pl.pallas_call(
        functools.partial(whole_kernel, n, c),
        out_shape=(
            jax.ShapeDtypeStruct((count, width), f32),
            jax.ShapeDtypeStruct((2, 1, vis), f32),
        ),
        in_specs=[anywhere, pl.BlockSpec(memory_space=pltpu.SMEM)] + [anywhere] * 10,
        out_specs=(vm, vm),
        scratch_shapes=[
            V((count, width), f32),
            V((2, 1, vis), f32),
            V((2, 1, vis), f32),
            V((n // 2 * TILE, width), half_t),
            V((2, 4 * LANES, 2 * LANES), half_t),
            V((2, 6 * LANES, 2 * LANES), half_t),
            V((tall, count), f32),
            V((count, tall), f32),
            dma((11,)),
            V((width, width), half_t),
            V((width, width), half_t),
            V((half, 2 * vis), half_t),
            V((2 * count, 2 * vis), half_t),
            V((1, 2 * vis), jnp.int32),
            V((1, 2 * vis), f32),
            V((2, 1, 2 * vis), f32),
            V((2, 1, 2 * vis), f32),
            V((2, 1, vis), f32),
            V((1, 2 * vis), jnp.int32),
            V((1, 2 * vis), jnp.int32),
            V((1, 2 * vis), jnp.int32),
            V((half // 2, 2 * vis), half_t),
            V((2, n, part + TILE, count), half_t),
            V((2, n, part + TILE, count), half_t),
            V((2, n, part, count), half_t),
            V((2, n, part, count), half_t),
            V((n, TILE, count), half_t),
            V((n, TILE, count), half_t),
            V((2 * count, half), half_t),
            V((width, count), half_t),
            V((width, count), half_t),
            V((tall, width + 2 * LANES), f32),
            V((2, EDGE, width), f32),
            V((count, width), f32),
            V((count, width), half_t),
            V((c, count, width // c), half_t),
            V((c, count, width // c), half_t),
            V((count, width + 4 * LANES), f32),
            V((tall, width), f32),
            V((2, EDGE, width), f32),
            dma((2, n)), dma((2, n)), dma((2, n)), dma((2, n)), dma((2,)), dma((2,)),
            dma((c,)), dma((c,)), dma((c,)), dma((c,)), dma((2,)), dma((2,)),
            dma((4,)), dma((4,)), dma((n,)), dma((n,)),
        ],
        compiler_params=pltpu.CompilerParams(
            collective_id=0, has_side_effects=True, vmem_limit_bytes=60 * 1024 * 1024
        ),
    )(
        image[0], margin, cells, weights, observed, dual_start,
        owner_table(n, count, width), edge_table(n, count, width),
        in_two(analysis_map()), in_two(synthesis_map()),
        row_map, np.ascontiguousarray(row_map.T),
    )
    return (fresh[None], dual)


def solution(mesh):
    n, c = mesh.shape["slab"], mesh.shape["chan"]

    def local(image, *rest):
        count, width = image.shape[1], image.shape[2]
        fits = n == 8 and count == LANES and width == n * count and width % (c * LANES) == 0
        if fits and rest[1].shape[1] % CHUNK == 0:
            return local_kernel(n, c, image, *rest)
        return local_plain(image, *rest)

    in_specs = (
        P("chan", "slab", None),
        P("slab"),
        P("chan", "slab"),
        P("chan", "slab"),
        P(None, "chan", "slab"),
        P(None, "chan", "slab"),
    )
    out_specs = (P("chan", "slab", None), P(None, "chan", "slab"))
    return jax.shard_map(local, mesh=mesh, in_specs=in_specs, out_specs=out_specs, check_vma=False)
```

```python
import functools
import math

import jax
import jax.numpy as jnp
import numpy as np
from jax import lax
from jax.experimental import pallas as pl
from jax.experimental.pallas import tpu as pltpu
from jax.sharding import PartitionSpec as P

N = 1024
HALO = 3


low_taps = (
    -0.010597401784997278,
    0.032883011666982945,
    0.030841381835986965,
    -0.18703481171888114,
    -0.02798376941698385,
    0.6308807679295904,
    0.7148465705525415,
    0.23037781330885523,
)
high_taps = (
    -0.23037781330885523,
    0.7148465705525415,
    -0.6308807679295904,
    -0.02798376941698385,
    0.18703481171888114,
    0.030841381835986965,
    -0.032883011666982945,
    -0.010597401784997278,
)
tau_step = 0.5
bound_level = 3.0
leading = (((0,), (0,)), ((), ()))


def with_halo(block, sides, width):
    for axis, dim in sides:
        count = lax.axis_size(axis)
        forward = [(i, i + 1) for i in range(count - 1)]
        backward = [(target, source) for source, target in forward]
        low = lax.ppermute(
            lax.slice_in_dim(block, block.shape[dim] - width, None, axis=dim), axis, forward
        )
        high = lax.ppermute(lax.slice_in_dim(block, 0, width, axis=dim), axis, backward)
        block = jnp.concatenate([low, block, high], axis=dim)
    return block


def tap_value(offset, taps):
    total = jnp.zeros(offset.shape, jnp.float32)
    for position in range(8):
        total = total + jnp.where(offset == position, taps[position], 0.0).astype(jnp.float32)
    return total


def fourier_tables(length):
    index = jnp.arange(length, dtype=jnp.int32)
    product = index[:, None] * index[None, :] % length
    angle = product.astype(jnp.float32) * (2.0 * math.pi / length)
    scale = 1.0 / math.sqrt(length)
    return (
        (jnp.cos(angle) * scale).astype(jnp.bfloat16),
        (jnp.sin(angle) * scale).astype(jnp.bfloat16),
    )


def row_matrix(count):
    half = count // 2
    line = jnp.arange(count + 2 * HALO, dtype=jnp.int32)[:, None]
    column = jnp.arange(count, dtype=jnp.int32)[None, :]
    offset = line - 2 * (column % half)
    return jnp.where(column < half, tap_value(offset, low_taps), tap_value(offset, high_taps))


def facet_mask(count, width):
    line = jnp.arange(count + 2 * HALO, dtype=jnp.int32)
    distance = jnp.maximum(jnp.maximum(HALO - line, line - count - HALO + 1), 0)
    return (distance[None, :] <= width[:, None]).astype(jnp.float32)


def column_forward(values):
    width = values.shape[1]
    half = width // 2
    padded = jnp.pad(values, ((0, 0), (HALO, 8)))
    even_cells = padded[:, 0::2]
    odd_cells = padded[:, 1::2]
    low_part = jnp.zeros((values.shape[0], half), jnp.float32)
    high_part = jnp.zeros((values.shape[0], half), jnp.float32)
    for position in range(8):
        source = even_cells if position % 2 == 0 else odd_cells
        piece = source[:, position // 2 : position // 2 + half]
        low_part = low_part + low_taps[position] * piece
        high_part = high_part + high_taps[position] * piece
    return jnp.concatenate([low_part, high_part], axis=1)


def column_adjoint(coefs):
    width = coefs.shape[1]
    half = width // 2
    low_part = coefs[:, :half]
    high_part = coefs[:, half:]
    even_sums = jnp.zeros((coefs.shape[0], half + 4), jnp.float32)
    odd_sums = jnp.zeros((coefs.shape[0], half + 4), jnp.float32)
    for position in range(8):
        term = low_taps[position] * low_part + high_taps[position] * high_part
        placed = jnp.pad(term, ((0, 0), (position // 2, 4 - position // 2)))
        if position % 2 == 0:
            even_sums = even_sums + placed
        else:
            odd_sums = odd_sums + placed
    joined = jnp.stack([even_sums, odd_sums], axis=2).reshape(coefs.shape[0], width + 8)
    return joined[:, HALO : HALO + width]


def data_part(lifted, dual, seen, places, gains, cos_table, sin_table):
    flat_b = lifted.astype(jnp.bfloat16)
    spectra = jnp.stack(
        [
            jnp.dot(flat_b, cos_table, preferred_element_type=jnp.float32),
            -jnp.dot(flat_b, sin_table, preferred_element_type=jnp.float32),
        ]
    ).astype(jnp.bfloat16)
    columns = lax.all_to_all(spectra, "slab", split_axis=2, concat_axis=1, tiled=True)
    grid_real = lax.dot_general(
        columns[0], cos_table, leading, preferred_element_type=jnp.float32
    ) + lax.dot_general(columns[1], sin_table, leading, preferred_element_type=jnp.float32)
    grid_imag = lax.dot_general(
        columns[1], cos_table, leading, preferred_element_type=jnp.float32
    ) - lax.dot_general(columns[0], sin_table, leading, preferred_element_type=jnp.float32)
    model = jnp.stack(
        [gains * grid_real.reshape(-1)[places], gains * grid_imag.reshape(-1)[places]]
    )
    fresh_dual = (dual + (model - seen)) / 2.0
    weighted = gains[None, :] * fresh_dual
    cell_count = grid_real.size
    hold_real = (
        jnp.zeros((cell_count,), jnp.float32)
        .at[places]
        .add(weighted[0])
        .reshape(grid_real.shape)
        .astype(jnp.bfloat16)
    )
    hold_imag = (
        jnp.zeros((cell_count,), jnp.float32)
        .at[places]
        .add(weighted[1])
        .reshape(grid_real.shape)
        .astype(jnp.bfloat16)
    )
    backward = jnp.stack(
        [
            jnp.dot(hold_real, cos_table, preferred_element_type=jnp.float32)
            - jnp.dot(hold_imag, sin_table, preferred_element_type=jnp.float32),
            jnp.dot(hold_real, sin_table, preferred_element_type=jnp.float32)
            + jnp.dot(hold_imag, cos_table, preferred_element_type=jnp.float32),
        ]
    ).astype(jnp.bfloat16)
    returned = lax.all_to_all(backward, "slab", split_axis=2, concat_axis=1, tiled=True)
    data_term = lax.dot_general(
        returned[0], cos_table, leading, preferred_element_type=jnp.float32
    ) - lax.dot_general(returned[1], sin_table, leading, preferred_element_type=jnp.float32)
    return (data_term, fresh_dual)


def wave_part(lifted, row_map, mask):
    highest = lax.Precision.HIGHEST
    count = lifted.shape[0]
    extended = with_halo(lifted, (("slab", 0),), HALO) * mask
    filtered = column_forward(extended)
    coef = lax.dot_general(
        row_map, filtered, leading, precision=highest, preferred_element_type=jnp.float32
    )
    squares = coef * coef
    share = lax.psum_scatter(
        squares.astype(jnp.bfloat16), "chan", scatter_dimension=1, tiled=True
    ).astype(jnp.float32)
    partial_factor = bound_level / jnp.maximum(jnp.sqrt(share), bound_level)
    factor = lax.all_gather(partial_factor, "chan", axis=1, tiled=True)
    fresh_dual = coef * factor
    back = column_adjoint(fresh_dual)
    spread = jnp.dot(row_map, back, precision=highest, preferred_element_type=jnp.float32) * mask
    bands = jnp.concatenate([spread[:HALO], spread[count + HALO :]], axis=0)
    arrived = with_halo(bands, (("slab", 0),), HALO)
    inner = spread[HALO : count + HALO]
    inner = inner.at[:HALO].add(arrived[:HALO])
    inner = inner.at[count - HALO :].add(arrived[3 * HALO :])
    return (inner, fresh_dual)


def local_plain(image, margin, cells, weights, observed, dual_start):
    count = image.shape[1]
    cos_table, sin_table = fourier_tables(N)
    row_map = row_matrix(count)
    mask = facet_mask(count, margin)[0][:, None]
    places = cells[0]
    gains = weights[0]
    seen = observed[:, 0, :]
    dual = dual_start[:, 0, :]
    estimate = image[0]
    data_term, dual = data_part(estimate, dual, seen, places, gains, cos_table, sin_table)
    wave_term, wave_dual = wave_part(estimate, row_map, mask)
    fresh = jnp.maximum(estimate - tau_step * (data_term + wave_term), 0.0)
    return (fresh[None], dual[:, None, :])


LANES = 128
EDGE = 8
CHUNK = 1024
TILE = 16
highest = lax.Precision.HIGHEST
crossed = (((1,), (1,)), ((), ()))


def pick(offset, taps):
    inside = (offset >= 0) & (offset < 8)
    return np.where(inside, np.asarray(taps, np.float64)[np.clip(offset, 0, 7)], 0.0)


def both_taps(offset, is_low):
    return np.where(is_low, pick(offset, low_taps), pick(offset, high_taps)).astype(np.float32)


def wave_rows(lines, length, span):
    angle = lines[:, None] * np.arange(span)[None, :] % length * (2.0 * np.pi / length)
    scale = 1.0 / np.sqrt(length)
    return np.cos(angle) * scale, -np.sin(angle) * scale


def first_column(owner, n, count):
    return count * owner if owner < n // 2 else count * (n - 1 - owner) + count // 2


def owner_table(n, count, width):
    blocks = []
    few = count // 4
    for h in range(2):
        for owner in range(n):
            lines = first_column(owner, n, count) + h * few + np.arange(few)
            blocks.extend(wave_rows(lines, width, width // 2))
    return np.concatenate(blocks).astype(np.float32).astype(jnp.bfloat16)


def edge_table(n, count, width):
    table = np.zeros((n // 2, TILE, width), np.float32)
    real, imag = wave_rows(count * (1 + np.arange(n // 2)), width, width)
    table[:, 0], table[:, TILE // 2] = real, imag
    return table.reshape(-1, width).astype(jnp.bfloat16)


def analysis_map():
    line = np.arange(4 * LANES)[:, None]
    column = np.arange(2 * LANES)[None, :]
    offset = line - (LANES - HALO) - 2 * (column % LANES)
    return both_taps(offset, column < LANES)


def synthesis_map():
    line = np.arange(6 * LANES)[:, None]
    column = np.arange(2 * LANES)[None, :]
    block = line // (2 * LANES) - 1
    offset = column - 2 * LANES * block - 2 * (line % LANES) + HALO
    return both_taps(offset, line % (2 * LANES) < LANES)


def wide_row_map(count):
    half = count // 2
    line = np.arange(count + 2 * EDGE)[:, None] - (EDGE - HALO)
    column = np.arange(count)[None, :]
    offset = line - 2 * (column % half)
    return both_taps(offset, column < half)


def in_two(values):
    top = values.astype(jnp.bfloat16)
    return np.stack([top, (values - top.astype(np.float32)).astype(jnp.bfloat16)])


def split(value):
    top = value.astype(jnp.bfloat16)
    return top, (value - top.astype(jnp.float32)).astype(jnp.bfloat16)


def fine_dot(left, right):
    total = jnp.dot(left[0], right[0], preferred_element_type=jnp.float32)
    total = total + jnp.dot(left[1], right[0], preferred_element_type=jnp.float32)
    return total + jnp.dot(left[0], right[1], preferred_element_type=jnp.float32)


def flip(place, bits):
    result = place
    for bit in (1, 2, 4):
        if bits & bit:
            result = result + bit - 2 * bit * (place // bit % 2)
    return result


def iota(shape, dim):
    return lax.broadcasted_iota(jnp.int32, shape, dim)


def whole_kernel(
    n, c, img_far, margin_far, cells, gains, seen_far, dual_far,
    half_far, edge_far, m1_far, m2_far, rows_far, rows_t_far,
    out, vout,
    margin, img, seen, dual, edge, m1, m2, rows, rows_t, fetched,
    af, bf, hot, marks, cset, gset, dset, vset, vback, rel_of, mod_of, fold_of, warm,
    send1, recv1, send2, recv2, send3, recv3, grid, bft,
    padded, halo, coef, sq, sq_in, totals, cpad, spread, bands,
    sa, ra, sb, rb, sh, rh, ss, rs, st, rt, sd, rd, sv, rv, sw, rw,
):
    me = lax.axis_index("slab")
    ch = lax.axis_index("chan")
    count, width = img.shape
    vis = cells.shape[1]
    part, half, side, few = count // 2, width // 2, n // 2, count // 4
    tall = count + 2 * EDGE
    pair = 2 * LANES
    block = width // c
    after, before, mate = lax.rem(me + 1, n), lax.rem(me + n - 1, n), n - 1 - me
    upper = me // side
    own = pl.ds(pl.multiple_of(upper * vis, vis), vis)
    other = pl.ds(pl.multiple_of((1 - upper) * vis, vis), vis)
    f32, bf16 = jnp.float32, jnp.bfloat16

    barrier = pltpu.get_barrier_semaphore()
    for d in range(1, n):
        pl.semaphore_signal(
            barrier, inc=1, device_id={"slab": lax.rem(me + d, n)},
            device_id_type=pl.DeviceIdType.MESH,
        )
    for d in range(1, c):
        pl.semaphore_signal(
            barrier, inc=1, device_id={"chan": lax.rem(ch + d, c)},
            device_id_type=pl.DeviceIdType.MESH,
        )

    local = [
        (img_far, img), (half_far, af.at[:, :half]), (edge_far, edge),
        (cells, cset.at[:, own]), (gains, gset.at[:, own]), (seen_far, seen), (dual_far, dual),
        (margin_far, margin), (m1_far, m1), (rows_far, rows), (rows_t_far, rows_t), (m2_far, m2),
    ]
    fetches = [
        pltpu.make_async_copy(far, near, fetched.at[i]) for i, (far, near) in enumerate(local)
    ]
    for fetch in fetches:
        fetch.start()

    def remote(src, dst, s, r, where):
        return pltpu.make_async_remote_copy(
            src_ref=src, dst_ref=dst, send_sem=s, recv_sem=r, device_id=where,
            device_id_type=pl.DeviceIdType.MESH,
        )

    sends = []

    def launch(*args):
        copy = remote(*args)
        copy.start()
        sends.append(copy)
        return copy

    for fetch in fetches[:3]:
        fetch.wait()
    flip_row = (1 - 2 * (iota((count, half), 0) % 2)).astype(f32).astype(bf16)
    for j in range(n):
        here = slice(j * count, (j + 1) * count)
        af[here, half:] = af[here, :half] * flip_row

    flat_b = img[...].astype(bf16)
    send1[0, :, part:, :] = jnp.zeros((n, TILE, count), bf16)
    spec = lax.dot_general(edge[...], flat_b, crossed, preferred_element_type=f32).astype(bf16)
    for j in range(n):
        k = n - 1 - j
        send1[1, j, part:, :] = (
            spec[k * TILE : (k + 1) * TILE] if j >= side else jnp.zeros((TILE, count), bf16)
        )

    def spectra(h):
        spec = lax.dot_general(
            af[h * half : (h + 1) * half, :], flat_b, crossed, preferred_element_type=f32
        ).astype(bf16)
        for j in range(n):
            send1[h, j, :part, :] = spec[j * part : (j + 1) * part]

    def outward(h, src, peer, d, home):
        rows = part if h == 0 else part + TILE
        return remote(
            send1.at[h, src, :rows], recv1.at[h, home, :rows], sa.at[h, d], ra.at[h, home],
            {"slab": peer},
        )

    def scatter(h):
        for d in range(n - 1, 0, -1):
            peer = flip(me, d)
            copy = outward(h, peer, peer, d, me)
            copy.start()
            sends.append(copy)
        recv1[h, me] = send1[h, me]

    fetches[3].wait()
    spectra(0)
    spectra(1)
    pl.semaphore_wait(barrier, n + c - 2)
    launch(cset.at[:, own], cset.at[:, own], sv.at[0], rv.at[0], {"slab": mate})
    up = launch(img.at[count - EDGE :], halo.at[0], sh.at[0], rh.at[0], {"slab": after})
    down = launch(img.at[:EDGE], halo.at[1], sh.at[1], rh.at[1], {"slab": before})
    scatter(0)
    scatter(1)
    for fetch in fetches[4:7]:
        fetch.wait()
    dset[:, :, own] = dual[...] - seen[...]
    launch(gset.at[:, own], gset.at[:, own], sv.at[1], rv.at[1], {"slab": mate})
    launch(dset.at[:, :, own], dset.at[:, :, own], sv.at[2], rv.at[2], {"slab": mate})

    def locate(here, sign):
        spot = cset[:, here]
        column, line = spot // width, spot % width
        column = jnp.where(sign > 0, column, count - column) - part * upper
        line = jnp.where((sign > 0) | (line == 0), line, width - line)
        rel_of[:, here] = jnp.where(column >= part + upper, -1, column)
        mod_of[:, here] = line
        fold = jnp.where(line > half, width - line, jnp.where(line == half, 0, line))
        fold_of[:, here] = fold

    step = 32

    def heat(here):
        fold = fold_of[:, here]

        def body(i, carry):
            hit = jnp.where(iota((step, vis), 0) + i * step == fold, 1.0, 0.0).astype(bf16)
            hot[pl.ds(pl.multiple_of(i * step, step), step), here] = hit
            return carry

        lax.fori_loop(0, half // step, body, 0)

        def merge(i, carry):
            top = pl.ds(pl.multiple_of(i * step, step), step)
            low = pl.ds(pl.multiple_of(half // 2 + i * step, step), step)
            warm[top, here] = hot[top, here] + hot[low, here]
            return carry

        lax.fori_loop(0, half // 2 // step, merge, 0)

    locate(own, 1 - 2 * upper)
    heat(own)


    for fetch in fetches[7:]:
        fetch.wait()
    reach = margin[0]

    def keep(shape, dim):
        line = iota(shape, dim)
        distance = jnp.maximum(jnp.maximum(EDGE - line, line - count - EDGE + 1), 0)
        return jnp.where(distance <= reach, 1.0, 0.0)

    row_fwd = split(rows_t[...] * keep((count, tall), 1))
    row_adj = split(rows[...] * keep((tall, count), 0))

    flip_lane = (1 - 2 * (iota((few, half), 1) % 2)).astype(f32).astype(bf16)
    nyquist = (1 - 2 * (iota((few, LANES), 0) % 2)).astype(f32) * (1.0 / math.sqrt(width))
    first_lane = iota((few, LANES), 1) == 0
    for j in range(2 * n):
        top = first_column(j % n, n, count) + j // n * few
        cosine = af[j * part : j * part + few, :half]
        sine = -af[j * part + few : (j + 1) * part, :half]
        mixed = jnp.where(first_lane, nyquist, sine[:, :LANES].astype(f32)).astype(bf16)
        for low, value in ((top, None), (half + top, flip_lane)):
            here = slice(low, low + few)
            bf[here, :half] = cosine if value is None else cosine * value
            rest = sine if value is None else sine * value
            bf[here, half : half + LANES] = (
                mixed if value is None else mixed * value[:, :LANES]
            )
            bf[here, half + LANES :] = rest[:, LANES:]
        bft[top : top + few, :] = af[j * part : j * part + few, :]
        bft[half + top : half + top + few, :] = -af[j * part + few : (j + 1) * part, :]
    pole = (1 - 2 * (iota((TILE, width), 1) % 2)).astype(f32) * (1.0 / math.sqrt(width))
    first_row = iota((TILE, width), 0) == 0
    bft[half : half + TILE, :] = jnp.where(
        first_row, pole, bft[half : half + TILE, :].astype(f32)
    ).astype(bf16)

    padded[:, :LANES] = jnp.zeros((tall, LANES), f32)
    padded[:, LANES + width :] = jnp.zeros((tall, LANES), f32)
    padded[EDGE : EDGE + count, LANES : LANES + width] = img[...]
    up.wait_recv()
    down.wait_recv()
    padded[:EDGE, LANES : LANES + width] = jnp.where(me > 0, halo[0], 0.0)
    padded[EDGE + count :, LANES : LANES + width] = jnp.where(me < n - 1, halo[1], 0.0)
    for b in range(width // pair):
        filtered = fine_dot(split(padded[:, b * pair : b * pair + 4 * LANES]), m1)
        piece = fine_dot(row_fwd, split(filtered))
        coef[:, b * pair : (b + 1) * pair] = piece
        sq[:, b * pair : (b + 1) * pair] = (piece * piece).astype(bf16)

    def slot(who):
        return pl.ds(pl.multiple_of(who * block, block), block)

    for d in range(1, c):
        peer = lax.rem(ch + d, c)
        launch(sq.at[:, slot(peer)], sq_in.at[ch], ss.at[d], rs.at[ch], {"chan": peer})

    remote(cset.at[:, other], cset.at[:, other], sv.at[0], rv.at[0], {"slab": mate}).wait_recv()
    locate(other, 2 * upper - 1)
    heat(other)

    def arrive(h):
        for d in range(n - 1, 0, -1):
            src = flip(me, d)
            outward(h, src, src, d, src).wait_recv()
        rows = part if h == 0 else part + TILE
        columns = jnp.concatenate([recv1[h, j, :rows] for j in range(n)], axis=1)
        value = jnp.dot(columns, bf[...], preferred_element_type=f32)
        planes = []
        for lanes in (slice(0, half), slice(half, width)):
            for k in range(2):
                planes.append(value[k * few : (k + 1) * few, lanes])
                if h == 1:
                    planes.append(value[part + k * EDGE : part + (k + 1) * EDGE, lanes])
        rows = sum(plane.shape[0] for plane in planes)
        grid[:rows] = jnp.concatenate(planes, axis=0).astype(bf16)

    def factors(line, sign):
        even = jnp.where(line == half, 0.0, 1.0)
        odd = jnp.where(line > half, -1.0, 1.0)
        odd = jnp.where((line == half) | (line == 0), 0.0, odd)
        return even, odd, 1.0 - even

    def spread_out(line, gain, fresh, sign):
        even, odd, last = factors(line, sign)
        real, imag = gain * fresh[0], gain * fresh[1] * sign
        return even * real, even * imag, last * real - odd * imag, odd * real + last * imag

    def visit(h, base, sign, i, carry):
        here = pl.ds(pl.multiple_of(base * vis + i * CHUNK, CHUNK), CHUNK)
        deep = few + h * EDGE
        found = jnp.dot(grid[: 4 * deep], hot[:, here], preferred_element_type=f32)
        rel = rel_of[:, here] - h * few
        match = iota((deep, CHUNK), 0) == rel
        c_re, c_im, s_re, s_im = [
            jnp.sum(
                jnp.where(match, found[k * deep : (k + 1) * deep], 0.0), axis=0, keepdims=True
            )
            for k in range(4)
        ]
        line = mod_of[:, here]
        gain = gset[:, here]
        even, odd, last = factors(line, sign)
        real = even * c_re + odd * s_im + last * s_re
        imag = (even * c_im - odd * s_re + last * s_im) * sign
        fresh = []
        for k, model in enumerate((real, imag)):
            fresh.append((dset[k, :, here] + gain * model) / 2.0)
            vset[k, :, here] = (
                fresh[k] if h == 0 else jnp.where(rel >= 0, fresh[k], vset[k, :, here])
            )
        late = fold_of[:, here] >= half // 2
        values = spread_out(line, gain, fresh, sign)
        for v in range(2):
            near = iota((few, CHUNK), 0) == jnp.where(late == (v == 1), rel, -1)
            for k, mark in enumerate(values):
                low = (v * 4 + k) * few
                marks[low : low + few, here] = jnp.where(near, mark, 0.0).astype(bf16)
        return carry

    facing = (1 - 2 * upper).astype(f32)
    def inward(h, src, peer, d, home):
        return remote(
            send2.at[h, src], recv2.at[h, home], sb.at[h, d], rb.at[h, home], {"slab": peer}
        )

    def give(h, bits):
        for d in bits:
            peer = flip(me, d)
            copy = inward(h, peer, peer, d, me)
            copy.start()
            sends.append(copy)

    for h in range(2):
        arrive(h)
        if h == 0:
            here_first = functools.partial(visit, h, upper, facing)
            lax.fori_loop(0, vis // CHUNK, here_first, 0, unroll=2)
            for d in range(1, c):
                src = lax.rem(ch + d, c)
                remote(sq.at[:, slot(src)], sq_in.at[src], ss.at[d], rs.at[src], {"chan": src}).wait_recv()
            total = sq[:, slot(ch)].astype(f32)
            for d in range(1, c):
                total = total + sq_in[lax.rem(ch + d, c)].astype(f32)
            totals[ch] = total.astype(bf16)
            for d in range(1, c):
                peer = lax.rem(ch + d, c)
                launch(totals.at[ch], totals.at[ch], st.at[d], rt.at[ch], {"chan": peer})
            remote(
                gset.at[:, other], gset.at[:, other], sv.at[1], rv.at[1], {"slab": mate}
            ).wait_recv()
            remote(
                dset.at[:, :, other], dset.at[:, :, other], sv.at[2], rv.at[2], {"slab": mate}
            ).wait_recv()
        else:
            here_first = functools.partial(visit, h, upper, facing)
            lax.fori_loop(0, vis // CHUNK, here_first, 0, unroll=2)
        there = functools.partial(visit, h, 1 - upper, -facing)
        lax.fori_loop(0, vis // CHUNK, there, 0, unroll=2)
        if h == 1:
            launch(vset.at[:, :, other], vback, sv.at[3], rv.at[3], {"slab": mate})
        held = lax.dot_general(
            marks[...], warm[...], crossed, preferred_element_type=f32
        ).astype(bf16)
        quarters = [held[low : low + part] for low in (0, count, part, count + part)]
        back = jnp.dot(
            jnp.concatenate(quarters, axis=1), bft[...], preferred_element_type=f32
        ).astype(bf16)
        for j in range(n):
            send2[h, j] = back[:, j * count : (j + 1) * count]
        give(h, range(n - 1, 0, -1))
        recv2[h, me] = send2[h, me]

    coarse, fine = half // 32, 32

    def outer(i, carry):
        here = pl.ds(pl.multiple_of(vis + i * CHUNK, CHUNK), CHUNK)
        line = mod_of[:, here]
        fold = jnp.where(line > half, width - line, jnp.where(line == half, 0, line))
        fresh = [vset[0, :, here], vset[1, :, here]]
        left = jnp.where(iota((coarse, CHUNK), 0) == fold // fine, 1.0, 0.0).astype(bf16)
        match = (iota((fine, CHUNK), 0) == fold % fine) & (rel_of[:, here] == part)
        right = jnp.concatenate(
            [
                jnp.where(match, mark, 0.0).astype(bf16)
                for mark in spread_out(line, gset[:, here], fresh, -1.0)
            ],
            axis=0,
        )
        return carry + lax.dot_general(right, left, crossed, preferred_element_type=f32)

    edges = lax.fori_loop(0, vis // CHUNK, outer, jnp.zeros((4 * fine, coarse), f32))
    lane = iota((coarse, half), 1)
    grow = jnp.where(lane // fine == iota((coarse, half), 0), 1.0, 0.0).astype(bf16)
    grown = jnp.dot(edges.astype(bf16), grow, preferred_element_type=f32)
    lane, line = iota((4 * fine, half), 1), iota((4 * fine, half), 0)
    grown = jnp.where(lane % fine == line % fine, grown, 0.0).astype(bf16)
    line, lane = iota((TILE, 4 * fine), 0), iota((TILE, 4 * fine), 1) // fine
    rows_of = []
    for k in range(2):
        gather = jnp.where(line == EDGE * (lane - 2 * k), 1.0, 0.0).astype(bf16)
        rows_of.append(jnp.dot(gather, grown, preferred_element_type=f32).astype(bf16))
    tails = jnp.dot(
        jnp.concatenate(rows_of, axis=1), bft[...], preferred_element_type=f32
    ).astype(bf16)
    for j in range(n):
        send3[j] = tails[:, j * count : (j + 1) * count]
    for d in range(n - 1, 0, -1):
        peer = flip(me, d)
        launch(send3.at[peer], recv3.at[me], sw.at[d], rw.at[me], {"slab": peer})
    recv3[me] = send3[me]

    for d in range(1, c):
        src = lax.rem(ch + d, c)
        remote(totals.at[src], totals.at[src], st.at[d], rt.at[src], {"chan": src}).wait_recv()
    cpad[:, :pair] = jnp.zeros((count, pair), f32)
    cpad[:, pair + width :] = jnp.zeros((count, pair), f32)
    for j in range(c):
        here = slice(j * block, (j + 1) * block)
        factor = bound_level / jnp.maximum(jnp.sqrt(totals[j].astype(f32)), bound_level)
        cpad[:, pair + j * block : pair + (j + 1) * block] = coef[:, here] * factor
    for b in range(width // pair):
        back = fine_dot(split(cpad[:, b * pair : b * pair + 6 * LANES]), m2)
        spread[:, b * pair : (b + 1) * pair] = fine_dot(row_adj, split(back))
    over = launch(spread.at[count + EDGE :], bands.at[0], sd.at[0], rd.at[0], {"slab": after})
    under = launch(spread.at[:EDGE], bands.at[1], sd.at[1], rd.at[1], {"slab": before})

    remote(vset.at[:, :, other], vback, sv.at[3], rv.at[3], {"slab": mate}).wait_recv()
    mine = rel_of[:, own] >= 0
    for k in range(2):
        vout[k] = jnp.where(mine, vset[k, :, own], vback[k])

    term = None
    for h in range(2):
        for d in range(n - 1, 0, -1):
            src = flip(me, d)
            inward(h, src, src, d, src).wait_recv()
        row = jnp.concatenate([recv2[h, j] for j in range(n)], axis=0)
        more = lax.dot_general(
            row, af[h * half : (h + 1) * half, :], leading, preferred_element_type=f32
        )
        term = more if term is None else term + more
    for d in range(n - 1, 0, -1):
        src = flip(me, d)
        remote(send3.at[src], recv3.at[src], sw.at[d], rw.at[src], {"slab": src}).wait_recv()
    tails = jnp.concatenate([recv3[n - 1 - k] for k in range(side)], axis=0)
    term = term + lax.dot_general(tails, edge[...], leading, preferred_element_type=f32)
    over.wait_recv()
    under.wait_recv()
    wave_first = spread[EDGE : 2 * EDGE, :] + jnp.where(me > 0, bands[0], 0.0)
    wave_last = spread[count : count + EDGE, :] + jnp.where(me < n - 1, bands[1], 0.0)
    wave = jnp.concatenate(
        [wave_first, spread[2 * EDGE : count, :], wave_last], axis=0
    )
    out[...] = jnp.maximum(img[...] - tau_step * (term + wave), 0.0)

    for copy in sends:
        copy.wait_send()


def local_kernel(n, c, image, margin, cells, weights, observed, dual_start):
    count, width = image.shape[1], image.shape[2]
    vis = cells.shape[1]
    tall = count + 2 * EDGE
    part, half = count // 2, width // 2
    half_t, f32 = jnp.bfloat16, jnp.float32
    V = pltpu.VMEM
    dma = pltpu.SemaphoreType.DMA
    row_map = wide_row_map(count)
    vm = pl.BlockSpec(memory_space=pltpu.VMEM)
    anywhere = pl.BlockSpec(memory_space=pl.ANY)
    fresh, dual = pl.pallas_call(
        functools.partial(whole_kernel, n, c),
        out_shape=(
            jax.ShapeDtypeStruct((count, width), f32),
            jax.ShapeDtypeStruct((2, 1, vis), f32),
        ),
        in_specs=[anywhere] * 12,
        out_specs=(vm, vm),
        scratch_shapes=[
            pltpu.SMEM((1,), jnp.int32),
            V((count, width), f32),
            V((2, 1, vis), f32),
            V((2, 1, vis), f32),
            V((n // 2 * TILE, width), half_t),
            V((2, 4 * LANES, 2 * LANES), half_t),
            V((2, 6 * LANES, 2 * LANES), half_t),
            V((tall, count), f32),
            V((count, tall), f32),
            dma((12,)),
            V((width, width), half_t),
            V((width, width), half_t),
            V((half, 2 * vis), half_t),
            V((2 * count, 2 * vis), half_t),
            V((1, 2 * vis), jnp.int32),
            V((1, 2 * vis), f32),
            V((2, 1, 2 * vis), f32),
            V((2, 1, 2 * vis), f32),
            V((2, 1, vis), f32),
            V((1, 2 * vis), jnp.int32),
            V((1, 2 * vis), jnp.int32),
            V((1, 2 * vis), jnp.int32),
            V((half // 2, 2 * vis), half_t),
            V((2, n, part + TILE, count), half_t),
            V((2, n, part + TILE, count), half_t),
            V((2, n, part, count), half_t),
            V((2, n, part, count), half_t),
            V((n, TILE, count), half_t),
            V((n, TILE, count), half_t),
            V((2 * count, half), half_t),
            V((width, width), half_t),
            V((tall, width + 2 * LANES), f32),
            V((2, EDGE, width), f32),
            V((count, width), f32),
            V((count, width), half_t),
            V((c, count, width // c), half_t),
            V((c, count, width // c), half_t),
            V((count, width + 4 * LANES), f32),
            V((tall, width), f32),
            V((2, EDGE, width), f32),
            dma((2, n)), dma((2, n)), dma((2, n)), dma((2, n)), dma((2,)), dma((2,)),
            dma((c,)), dma((c,)), dma((c,)), dma((c,)), dma((2,)), dma((2,)),
            dma((4,)), dma((4,)), dma((n,)), dma((n,)),
        ],
        compiler_params=pltpu.CompilerParams(
            collective_id=0, has_side_effects=True, vmem_limit_bytes=60 * 1024 * 1024
        ),
    )(
        image[0], margin, cells, weights, observed, dual_start,
        owner_table(n, count, width), edge_table(n, count, width),
        in_two(analysis_map()), in_two(synthesis_map()),
        row_map, np.ascontiguousarray(row_map.T),
    )
    return (fresh[None], dual)


def solution(mesh):
    n, c = mesh.shape["slab"], mesh.shape["chan"]

    def local(image, *rest):
        count, width = image.shape[1], image.shape[2]
        fits = n == 8 and count == LANES and width == n * count and width % (c * LANES) == 0
        if fits and rest[1].shape[1] % CHUNK == 0:
            return local_kernel(n, c, image, *rest)
        return local_plain(image, *rest)

    in_specs = (
        P("chan", "slab", None),
        P("slab"),
        P("chan", "slab"),
        P("chan", "slab"),
        P(None, "chan", "slab"),
        P(None, "chan", "slab"),
    )
    out_specs = (P("chan", "slab", None), P(None, "chan", "slab"))
    return jax.shard_map(local, mesh=mesh, in_specs=in_specs, out_specs=out_specs, check_vma=False)
```

```python
import functools
import math

import jax
import jax.numpy as jnp
import numpy as np
from jax import lax
from jax.experimental import pallas as pl
from jax.experimental.pallas import tpu as pltpu
from jax.sharding import PartitionSpec as P

N = 1024
HALO = 3


low_taps = (
    -0.010597401784997278,
    0.032883011666982945,
    0.030841381835986965,
    -0.18703481171888114,
    -0.02798376941698385,
    0.6308807679295904,
    0.7148465705525415,
    0.23037781330885523,
)
high_taps = (
    -0.23037781330885523,
    0.7148465705525415,
    -0.6308807679295904,
    -0.02798376941698385,
    0.18703481171888114,
    0.030841381835986965,
    -0.032883011666982945,
    -0.010597401784997278,
)
tau_step = 0.5
bound_level = 3.0
leading = (((0,), (0,)), ((), ()))


def with_halo(block, sides, width):
    for axis, dim in sides:
        count = lax.axis_size(axis)
        forward = [(i, i + 1) for i in range(count - 1)]
        backward = [(target, source) for source, target in forward]
        low = lax.ppermute(
            lax.slice_in_dim(block, block.shape[dim] - width, None, axis=dim), axis, forward
        )
        high = lax.ppermute(lax.slice_in_dim(block, 0, width, axis=dim), axis, backward)
        block = jnp.concatenate([low, block, high], axis=dim)
    return block


def tap_value(offset, taps):
    total = jnp.zeros(offset.shape, jnp.float32)
    for position in range(8):
        total = total + jnp.where(offset == position, taps[position], 0.0).astype(jnp.float32)
    return total


def fourier_tables(length):
    index = jnp.arange(length, dtype=jnp.int32)
    product = index[:, None] * index[None, :] % length
    angle = product.astype(jnp.float32) * (2.0 * math.pi / length)
    scale = 1.0 / math.sqrt(length)
    return (
        (jnp.cos(angle) * scale).astype(jnp.bfloat16),
        (jnp.sin(angle) * scale).astype(jnp.bfloat16),
    )


def row_matrix(count):
    half = count // 2
    line = jnp.arange(count + 2 * HALO, dtype=jnp.int32)[:, None]
    column = jnp.arange(count, dtype=jnp.int32)[None, :]
    offset = line - 2 * (column % half)
    return jnp.where(column < half, tap_value(offset, low_taps), tap_value(offset, high_taps))


def facet_mask(count, width):
    line = jnp.arange(count + 2 * HALO, dtype=jnp.int32)
    distance = jnp.maximum(jnp.maximum(HALO - line, line - count - HALO + 1), 0)
    return (distance[None, :] <= width[:, None]).astype(jnp.float32)


def column_forward(values):
    width = values.shape[1]
    half = width // 2
    padded = jnp.pad(values, ((0, 0), (HALO, 8)))
    even_cells = padded[:, 0::2]
    odd_cells = padded[:, 1::2]
    low_part = jnp.zeros((values.shape[0], half), jnp.float32)
    high_part = jnp.zeros((values.shape[0], half), jnp.float32)
    for position in range(8):
        source = even_cells if position % 2 == 0 else odd_cells
        piece = source[:, position // 2 : position // 2 + half]
        low_part = low_part + low_taps[position] * piece
        high_part = high_part + high_taps[position] * piece
    return jnp.concatenate([low_part, high_part], axis=1)


def column_adjoint(coefs):
    width = coefs.shape[1]
    half = width // 2
    low_part = coefs[:, :half]
    high_part = coefs[:, half:]
    even_sums = jnp.zeros((coefs.shape[0], half + 4), jnp.float32)
    odd_sums = jnp.zeros((coefs.shape[0], half + 4), jnp.float32)
    for position in range(8):
        term = low_taps[position] * low_part + high_taps[position] * high_part
        placed = jnp.pad(term, ((0, 0), (position // 2, 4 - position // 2)))
        if position % 2 == 0:
            even_sums = even_sums + placed
        else:
            odd_sums = odd_sums + placed
    joined = jnp.stack([even_sums, odd_sums], axis=2).reshape(coefs.shape[0], width + 8)
    return joined[:, HALO : HALO + width]


def data_part(lifted, dual, seen, places, gains, cos_table, sin_table):
    flat_b = lifted.astype(jnp.bfloat16)
    spectra = jnp.stack(
        [
            jnp.dot(flat_b, cos_table, preferred_element_type=jnp.float32),
            -jnp.dot(flat_b, sin_table, preferred_element_type=jnp.float32),
        ]
    ).astype(jnp.bfloat16)
    columns = lax.all_to_all(spectra, "slab", split_axis=2, concat_axis=1, tiled=True)
    grid_real = lax.dot_general(
        columns[0], cos_table, leading, preferred_element_type=jnp.float32
    ) + lax.dot_general(columns[1], sin_table, leading, preferred_element_type=jnp.float32)
    grid_imag = lax.dot_general(
        columns[1], cos_table, leading, preferred_element_type=jnp.float32
    ) - lax.dot_general(columns[0], sin_table, leading, preferred_element_type=jnp.float32)
    model = jnp.stack(
        [gains * grid_real.reshape(-1)[places], gains * grid_imag.reshape(-1)[places]]
    )
    fresh_dual = (dual + (model - seen)) / 2.0
    weighted = gains[None, :] * fresh_dual
    cell_count = grid_real.size
    hold_real = (
        jnp.zeros((cell_count,), jnp.float32)
        .at[places]
        .add(weighted[0])
        .reshape(grid_real.shape)
        .astype(jnp.bfloat16)
    )
    hold_imag = (
        jnp.zeros((cell_count,), jnp.float32)
        .at[places]
        .add(weighted[1])
        .reshape(grid_real.shape)
        .astype(jnp.bfloat16)
    )
    backward = jnp.stack(
        [
            jnp.dot(hold_real, cos_table, preferred_element_type=jnp.float32)
            - jnp.dot(hold_imag, sin_table, preferred_element_type=jnp.float32),
            jnp.dot(hold_real, sin_table, preferred_element_type=jnp.float32)
            + jnp.dot(hold_imag, cos_table, preferred_element_type=jnp.float32),
        ]
    ).astype(jnp.bfloat16)
    returned = lax.all_to_all(backward, "slab", split_axis=2, concat_axis=1, tiled=True)
    data_term = lax.dot_general(
        returned[0], cos_table, leading, preferred_element_type=jnp.float32
    ) - lax.dot_general(returned[1], sin_table, leading, preferred_element_type=jnp.float32)
    return (data_term, fresh_dual)


def wave_part(lifted, row_map, mask):
    highest = lax.Precision.HIGHEST
    count = lifted.shape[0]
    extended = with_halo(lifted, (("slab", 0),), HALO) * mask
    filtered = column_forward(extended)
    coef = lax.dot_general(
        row_map, filtered, leading, precision=highest, preferred_element_type=jnp.float32
    )
    squares = coef * coef
    share = lax.psum_scatter(
        squares.astype(jnp.bfloat16), "chan", scatter_dimension=1, tiled=True
    ).astype(jnp.float32)
    partial_factor = bound_level / jnp.maximum(jnp.sqrt(share), bound_level)
    factor = lax.all_gather(partial_factor, "chan", axis=1, tiled=True)
    fresh_dual = coef * factor
    back = column_adjoint(fresh_dual)
    spread = jnp.dot(row_map, back, precision=highest, preferred_element_type=jnp.float32) * mask
    bands = jnp.concatenate([spread[:HALO], spread[count + HALO :]], axis=0)
    arrived = with_halo(bands, (("slab", 0),), HALO)
    inner = spread[HALO : count + HALO]
    inner = inner.at[:HALO].add(arrived[:HALO])
    inner = inner.at[count - HALO :].add(arrived[3 * HALO :])
    return (inner, fresh_dual)


def local_plain(image, margin, cells, weights, observed, dual_start):
    count = image.shape[1]
    cos_table, sin_table = fourier_tables(N)
    row_map = row_matrix(count)
    mask = facet_mask(count, margin)[0][:, None]
    places = cells[0]
    gains = weights[0]
    seen = observed[:, 0, :]
    dual = dual_start[:, 0, :]
    estimate = image[0]
    data_term, dual = data_part(estimate, dual, seen, places, gains, cos_table, sin_table)
    wave_term, wave_dual = wave_part(estimate, row_map, mask)
    fresh = jnp.maximum(estimate - tau_step * (data_term + wave_term), 0.0)
    return (fresh[None], dual[:, None, :])


LANES = 128
EDGE = 8
CHUNK = 1024
TILE = 16
highest = lax.Precision.HIGHEST
crossed = (((1,), (1,)), ((), ()))


def pick(offset, taps):
    inside = (offset >= 0) & (offset < 8)
    return np.where(inside, np.asarray(taps, np.float64)[np.clip(offset, 0, 7)], 0.0)


def both_taps(offset, is_low):
    return np.where(is_low, pick(offset, low_taps), pick(offset, high_taps)).astype(np.float32)


def wave_rows(lines, length, span):
    angle = lines[:, None] * np.arange(span)[None, :] % length * (2.0 * np.pi / length)
    scale = 1.0 / np.sqrt(length)
    return np.cos(angle) * scale, -np.sin(angle) * scale


def first_column(owner, n, count):
    return count * owner if owner < n // 2 else count * (n - 1 - owner) + count // 2


def owner_table(n, count, width):
    blocks = []
    few = count // 4
    for h in range(2):
        for owner in range(n):
            lines = first_column(owner, n, count) + h * few + np.arange(few)
            blocks.extend(wave_rows(lines, width, width // 2))
    return np.concatenate(blocks).astype(np.float32).astype(jnp.bfloat16)


def edge_table(n, count, width):
    table = np.zeros((n // 2, TILE, width), np.float32)
    real, imag = wave_rows(count * (1 + np.arange(n // 2)), width, width)
    table[:, 0], table[:, TILE // 2] = real, imag
    return table.reshape(-1, width).astype(jnp.bfloat16)


def analysis_map():
    line = np.arange(4 * LANES)[:, None]
    column = np.arange(2 * LANES)[None, :]
    offset = line - (LANES - HALO) - 2 * (column % LANES)
    return both_taps(offset, column < LANES)


def synthesis_map():
    line = np.arange(6 * LANES)[:, None]
    column = np.arange(2 * LANES)[None, :]
    block = line // (2 * LANES) - 1
    offset = column - 2 * LANES * block - 2 * (line % LANES) + HALO
    return both_taps(offset, line % (2 * LANES) < LANES)


def wide_row_map(count):
    half = count // 2
    line = np.arange(count + 2 * EDGE)[:, None] - (EDGE - HALO)
    column = np.arange(count)[None, :]
    offset = line - 2 * (column % half)
    return both_taps(offset, column < half)


def in_two(values):
    top = values.astype(jnp.bfloat16)
    return np.stack([top, (values - top.astype(np.float32)).astype(jnp.bfloat16)])


def split(value):
    top = value.astype(jnp.bfloat16)
    return top, (value - top.astype(jnp.float32)).astype(jnp.bfloat16)


def fine_dot(left, right):
    total = jnp.dot(left[0], right[0], preferred_element_type=jnp.float32)
    total = total + jnp.dot(left[1], right[0], preferred_element_type=jnp.float32)
    return total + jnp.dot(left[0], right[1], preferred_element_type=jnp.float32)


def flip(place, bits):
    result = place
    for bit in (1, 2, 4):
        if bits & bit:
            result = result + bit - 2 * bit * (place // bit % 2)
    return result


def iota(shape, dim):
    return lax.broadcasted_iota(jnp.int32, shape, dim)


def whole_kernel(
    n, c, img_far, margin_far, cells, gains, seen_far, dual_far,
    half_far, edge_far, m1_far, m2_far, rows_far, rows_t_far,
    out, vout,
    margin, img, seen, dual, edge, m1, m2, rows, rows_t, fetched,
    af, bf, hot, marks, cset, gset, dset, vset, vback, rel_of, mod_of, fold_of, warm,
    send1, recv1, send2, recv2, send3, recv3, grid, bft,
    padded, halo, coef, sq, sq_in, totals, cpad, spread, bands,
    sa, ra, sb, rb, sh, rh, ss, rs, st, rt, sd, rd, sv, rv, sw, rw,
):
    me = lax.axis_index("slab")
    ch = lax.axis_index("chan")
    count, width = img.shape
    vis = cells.shape[1]
    part, half, side, few = count // 2, width // 2, n // 2, count // 4
    tall = count + 2 * EDGE
    pair = 2 * LANES
    block = width // c
    after, before, mate = lax.rem(me + 1, n), lax.rem(me + n - 1, n), n - 1 - me
    upper = me // side
    own = pl.ds(pl.multiple_of(upper * vis, vis), vis)
    other = pl.ds(pl.multiple_of((1 - upper) * vis, vis), vis)
    f32, bf16 = jnp.float32, jnp.bfloat16

    barrier = pltpu.get_barrier_semaphore()
    for d in range(1, n):
        pl.semaphore_signal(
            barrier, inc=1, device_id={"slab": lax.rem(me + d, n)},
            device_id_type=pl.DeviceIdType.MESH,
        )
    for d in range(1, c):
        pl.semaphore_signal(
            barrier, inc=1, device_id={"chan": lax.rem(ch + d, c)},
            device_id_type=pl.DeviceIdType.MESH,
        )

    local = [
        (img_far, img), (half_far, af.at[:, :half]), (edge_far, edge),
        (cells, cset.at[:, own]), (gains, gset.at[:, own]), (seen_far, seen), (dual_far, dual),
        (margin_far, margin), (m1_far, m1), (rows_far, rows), (rows_t_far, rows_t), (m2_far, m2),
    ]
    fetches = [
        pltpu.make_async_copy(far, near, fetched.at[i]) for i, (far, near) in enumerate(local)
    ]
    for fetch in fetches:
        fetch.start()

    def remote(src, dst, s, r, where):
        return pltpu.make_async_remote_copy(
            src_ref=src, dst_ref=dst, send_sem=s, recv_sem=r, device_id=where,
            device_id_type=pl.DeviceIdType.MESH,
        )

    sends = []

    def launch(*args):
        copy = remote(*args)
        copy.start()
        sends.append(copy)
        return copy

    for fetch in fetches[:3]:
        fetch.wait()
    flip_row = (1 - 2 * (iota((count, half), 0) % 2)).astype(f32).astype(bf16)
    for j in range(n):
        here = slice(j * count, (j + 1) * count)
        af[here, half:] = af[here, :half] * flip_row

    flat_b = img[...].astype(bf16)
    send1[0, :, part:, :] = jnp.zeros((n, TILE, count), bf16)
    spec = lax.dot_general(edge[...], flat_b, crossed, preferred_element_type=f32).astype(bf16)
    for j in range(n):
        k = n - 1 - j
        send1[1, j, part:, :] = (
            spec[k * TILE : (k + 1) * TILE] if j >= side else jnp.zeros((TILE, count), bf16)
        )

    def spectra(h):
        spec = lax.dot_general(
            af[h * half : (h + 1) * half, :], flat_b, crossed, preferred_element_type=f32
        ).astype(bf16)
        for j in range(n):
            send1[h, j, :part, :] = spec[j * part : (j + 1) * part]

    def outward(h, src, peer, d, home):
        rows = part if h == 0 else part + TILE
        return remote(
            send1.at[h, src, :rows], recv1.at[h, home, :rows], sa.at[h, d], ra.at[h, home],
            {"slab": peer},
        )

    def scatter(h):
        for d in range(n - 1, 0, -1):
            peer = flip(me, d)
            copy = outward(h, peer, peer, d, me)
            copy.start()
            sends.append(copy)
        recv1[h, me] = send1[h, me]

    fetches[3].wait()
    spectra(0)
    spectra(1)
    pl.semaphore_wait(barrier, n + c - 2)
    up = launch(img.at[count - EDGE :], halo.at[0], sh.at[0], rh.at[0], {"slab": after})
    down = launch(img.at[:EDGE], halo.at[1], sh.at[1], rh.at[1], {"slab": before})
    scatter(0)
    launch(cset.at[:, own], cset.at[:, own], sv.at[0], rv.at[0], {"slab": mate})
    scatter(1)
    for fetch in fetches[4:7]:
        fetch.wait()
    dset[:, :, own] = dual[...] - seen[...]
    launch(gset.at[:, own], gset.at[:, own], sv.at[1], rv.at[1], {"slab": mate})
    launch(dset.at[:, :, own], dset.at[:, :, own], sv.at[2], rv.at[2], {"slab": mate})

    def locate(here, sign):
        spot = cset[:, here]
        column, line = spot // width, spot % width
        column = jnp.where(sign > 0, column, count - column) - part * upper
        line = jnp.where((sign > 0) | (line == 0), line, width - line)
        rel_of[:, here] = jnp.where(column >= part + upper, -1, column)
        mod_of[:, here] = line
        fold = jnp.where(line > half, width - line, jnp.where(line == half, 0, line))
        fold_of[:, here] = fold

    step = 32

    def heat(here):
        fold = fold_of[:, here]

        def body(i, carry):
            hit = jnp.where(iota((step, vis), 0) + i * step == fold, 1.0, 0.0).astype(bf16)
            hot[pl.ds(pl.multiple_of(i * step, step), step), here] = hit
            return carry

        lax.fori_loop(0, half // step, body, 0)

        def merge(i, carry):
            top = pl.ds(pl.multiple_of(i * step, step), step)
            low = pl.ds(pl.multiple_of(half // 2 + i * step, step), step)
            warm[top, here] = hot[top, here] + hot[low, here]
            return carry

        lax.fori_loop(0, half // 2 // step, merge, 0)

    locate(own, 1 - 2 * upper)
    heat(own)


    for fetch in fetches[7:]:
        fetch.wait()
    reach = margin[0]

    def keep(shape, dim):
        line = iota(shape, dim)
        distance = jnp.maximum(jnp.maximum(EDGE - line, line - count - EDGE + 1), 0)
        return jnp.where(distance <= reach, 1.0, 0.0)

    row_fwd = split(rows_t[...] * keep((count, tall), 1))
    row_adj = split(rows[...] * keep((tall, count), 0))

    flip_lane = (1 - 2 * (iota((few, half), 1) % 2)).astype(f32).astype(bf16)
    nyquist = (1 - 2 * (iota((few, LANES), 0) % 2)).astype(f32) * (1.0 / math.sqrt(width))
    first_lane = iota((few, LANES), 1) == 0
    for j in range(2 * n):
        top = first_column(j % n, n, count) + j // n * few
        cosine = af[j * part : j * part + few, :half]
        sine = -af[j * part + few : (j + 1) * part, :half]
        mixed = jnp.where(first_lane, nyquist, sine[:, :LANES].astype(f32)).astype(bf16)
        for low, value in ((top, None), (half + top, flip_lane)):
            here = slice(low, low + few)
            bf[here, :half] = cosine if value is None else cosine * value
            rest = sine if value is None else sine * value
            bf[here, half : half + LANES] = (
                mixed if value is None else mixed * value[:, :LANES]
            )
            bf[here, half + LANES :] = rest[:, LANES:]
        bft[top : top + few, :] = af[j * part : j * part + few, :]
        bft[half + top : half + top + few, :] = -af[j * part + few : (j + 1) * part, :]
    pole = (1 - 2 * (iota((TILE, width), 1) % 2)).astype(f32) * (1.0 / math.sqrt(width))
    first_row = iota((TILE, width), 0) == 0
    bft[half : half + TILE, :] = jnp.where(
        first_row, pole, bft[half : half + TILE, :].astype(f32)
    ).astype(bf16)

    padded[:, :LANES] = jnp.zeros((tall, LANES), f32)
    padded[:, LANES + width :] = jnp.zeros((tall, LANES), f32)
    padded[EDGE : EDGE + count, LANES : LANES + width] = img[...]
    up.wait_recv()
    down.wait_recv()
    padded[:EDGE, LANES : LANES + width] = jnp.where(me > 0, halo[0], 0.0)
    padded[EDGE + count :, LANES : LANES + width] = jnp.where(me < n - 1, halo[1], 0.0)
    for b in range(width // pair):
        filtered = fine_dot(split(padded[:, b * pair : b * pair + 4 * LANES]), m1)
        piece = fine_dot(row_fwd, split(filtered))
        coef[:, b * pair : (b + 1) * pair] = piece
        sq[:, b * pair : (b + 1) * pair] = (piece * piece).astype(bf16)

    def slot(who):
        return pl.ds(pl.multiple_of(who * block, block), block)

    for d in range(1, c):
        peer = lax.rem(ch + d, c)
        launch(sq.at[:, slot(peer)], sq_in.at[ch], ss.at[d], rs.at[ch], {"chan": peer})

    remote(cset.at[:, other], cset.at[:, other], sv.at[0], rv.at[0], {"slab": mate}).wait_recv()
    locate(other, 2 * upper - 1)
    heat(other)

    def arrive(h):
        for d in range(n - 1, 0, -1):
            src = flip(me, d)
            outward(h, src, src, d, src).wait_recv()
        rows = part if h == 0 else part + TILE
        columns = jnp.concatenate([recv1[h, j, :rows] for j in range(n)], axis=1)
        value = jnp.dot(columns, bf[...], preferred_element_type=f32)
        planes = []
        for lanes in (slice(0, half), slice(half, width)):
            for k in range(2):
                planes.append(value[k * few : (k + 1) * few, lanes])
                if h == 1:
                    planes.append(value[part + k * EDGE : part + (k + 1) * EDGE, lanes])
        rows = sum(plane.shape[0] for plane in planes)
        grid[:rows] = jnp.concatenate(planes, axis=0).astype(bf16)

    def factors(line, sign):
        even = jnp.where(line == half, 0.0, 1.0)
        odd = jnp.where(line > half, -1.0, 1.0)
        odd = jnp.where((line == half) | (line == 0), 0.0, odd)
        return even, odd, 1.0 - even

    def spread_out(line, gain, fresh, sign):
        even, odd, last = factors(line, sign)
        real, imag = gain * fresh[0], gain * fresh[1] * sign
        return even * real, even * imag, last * real - odd * imag, odd * real + last * imag

    def visit(h, base, sign, i, carry):
        here = pl.ds(pl.multiple_of(base * vis + i * CHUNK, CHUNK), CHUNK)
        deep = few + h * EDGE
        found = jnp.dot(grid[: 4 * deep], hot[:, here], preferred_element_type=f32)
        rel = rel_of[:, here] - h * few
        match = iota((deep, CHUNK), 0) == rel
        c_re, c_im, s_re, s_im = [
            jnp.sum(
                jnp.where(match, found[k * deep : (k + 1) * deep], 0.0), axis=0, keepdims=True
            )
            for k in range(4)
        ]
        line = mod_of[:, here]
        gain = gset[:, here]
        even, odd, last = factors(line, sign)
        real = even * c_re + odd * s_im + last * s_re
        imag = (even * c_im - odd * s_re + last * s_im) * sign
        fresh = []
        for k, model in enumerate((real, imag)):
            fresh.append((dset[k, :, here] + gain * model) / 2.0)
            vset[k, :, here] = (
                fresh[k] if h == 0 else jnp.where(rel >= 0, fresh[k], vset[k, :, here])
            )
        late = fold_of[:, here] >= half // 2
        values = spread_out(line, gain, fresh, sign)
        for v in range(2):
            near = iota((few, CHUNK), 0) == jnp.where(late == (v == 1), rel, -1)
            for k, mark in enumerate(values):
                low = (v * 4 + k) * few
                marks[low : low + few, here] = jnp.where(near, mark, 0.0).astype(bf16)
        return carry

    facing = (1 - 2 * upper).astype(f32)
    def inward(h, src, peer, d, home):
        return remote(
            send2.at[h, src], recv2.at[h, home], sb.at[h, d], rb.at[h, home], {"slab": peer}
        )

    def give(h, bits):
        for d in bits:
            peer = flip(me, d)
            copy = inward(h, peer, peer, d, me)
            copy.start()
            sends.append(copy)

    for h in range(2):
        arrive(h)
        if h == 0:
            here_first = functools.partial(visit, h, upper, facing)
            lax.fori_loop(0, vis // CHUNK, here_first, 0, unroll=2)
            for d in range(1, c):
                src = lax.rem(ch + d, c)
                remote(sq.at[:, slot(src)], sq_in.at[src], ss.at[d], rs.at[src], {"chan": src}).wait_recv()
            total = sq[:, slot(ch)].astype(f32)
            for d in range(1, c):
                total = total + sq_in[lax.rem(ch + d, c)].astype(f32)
            totals[ch] = total.astype(bf16)
            for d in range(1, c):
                peer = lax.rem(ch + d, c)
                launch(totals.at[ch], totals.at[ch], st.at[d], rt.at[ch], {"chan": peer})
            remote(
                gset.at[:, other], gset.at[:, other], sv.at[1], rv.at[1], {"slab": mate}
            ).wait_recv()
            remote(
                dset.at[:, :, other], dset.at[:, :, other], sv.at[2], rv.at[2], {"slab": mate}
            ).wait_recv()
        else:
            here_first = functools.partial(visit, h, upper, facing)
            lax.fori_loop(0, vis // CHUNK, here_first, 0, unroll=2)
        there = functools.partial(visit, h, 1 - upper, -facing)
        lax.fori_loop(0, vis // CHUNK, there, 0, unroll=2)
        if h == 1:
            launch(vset.at[:, :, other], vback, sv.at[3], rv.at[3], {"slab": mate})
        held = lax.dot_general(
            marks[...], warm[...], crossed, preferred_element_type=f32
        ).astype(bf16)
        quarters = [held[low : low + part] for low in (0, count, part, count + part)]
        back = jnp.dot(
            jnp.concatenate(quarters, axis=1), bft[...], preferred_element_type=f32
        ).astype(bf16)
        for j in range(n):
            send2[h, j] = back[:, j * count : (j + 1) * count]
        give(h, range(n - 1, 0, -1))
        recv2[h, me] = send2[h, me]

    coarse, fine = half // 32, 32

    def outer(i, carry):
        here = pl.ds(pl.multiple_of(vis + i * CHUNK, CHUNK), CHUNK)
        line = mod_of[:, here]
        fold = jnp.where(line > half, width - line, jnp.where(line == half, 0, line))
        fresh = [vset[0, :, here], vset[1, :, here]]
        left = jnp.where(iota((coarse, CHUNK), 0) == fold // fine, 1.0, 0.0).astype(bf16)
        match = (iota((fine, CHUNK), 0) == fold % fine) & (rel_of[:, here] == part)
        right = jnp.concatenate(
            [
                jnp.where(match, mark, 0.0).astype(bf16)
                for mark in spread_out(line, gset[:, here], fresh, -1.0)
            ],
            axis=0,
        )
        return carry + lax.dot_general(right, left, crossed, preferred_element_type=f32)

    edges = lax.fori_loop(0, vis // CHUNK, outer, jnp.zeros((4 * fine, coarse), f32))
    lane = iota((coarse, half), 1)
    grow = jnp.where(lane // fine == iota((coarse, half), 0), 1.0, 0.0).astype(bf16)
    grown = jnp.dot(edges.astype(bf16), grow, preferred_element_type=f32)
    lane, line = iota((4 * fine, half), 1), iota((4 * fine, half), 0)
    grown = jnp.where(lane % fine == line % fine, grown, 0.0).astype(bf16)
    line, lane = iota((TILE, 4 * fine), 0), iota((TILE, 4 * fine), 1) // fine
    rows_of = []
    for k in range(2):
        gather = jnp.where(line == EDGE * (lane - 2 * k), 1.0, 0.0).astype(bf16)
        rows_of.append(jnp.dot(gather, grown, preferred_element_type=f32).astype(bf16))
    tails = jnp.dot(
        jnp.concatenate(rows_of, axis=1), bft[...], preferred_element_type=f32
    ).astype(bf16)
    for j in range(n):
        send3[j] = tails[:, j * count : (j + 1) * count]
    for d in range(n - 1, 0, -1):
        peer = flip(me, d)
        launch(send3.at[peer], recv3.at[me], sw.at[d], rw.at[me], {"slab": peer})
    recv3[me] = send3[me]

    for d in range(1, c):
        src = lax.rem(ch + d, c)
        remote(totals.at[src], totals.at[src], st.at[d], rt.at[src], {"chan": src}).wait_recv()
    cpad[:, :pair] = jnp.zeros((count, pair), f32)
    cpad[:, pair + width :] = jnp.zeros((count, pair), f32)
    for j in range(c):
        here = slice(j * block, (j + 1) * block)
        factor = bound_level / jnp.maximum(jnp.sqrt(totals[j].astype(f32)), bound_level)
        cpad[:, pair + j * block : pair + (j + 1) * block] = coef[:, here] * factor
    for b in range(width // pair):
        near = cpad[:, b * pair : b * pair + 6 * LANES].astype(bf16)
        back = jnp.dot(near, m2[0], preferred_element_type=f32)
        back = back + jnp.dot(near, m2[1], preferred_element_type=f32)
        back_b = back.astype(bf16)
        spread[:, b * pair : (b + 1) * pair] = jnp.dot(
            row_adj[0], back_b, preferred_element_type=f32
        ) + jnp.dot(row_adj[1], back_b, preferred_element_type=f32)
    over = launch(spread.at[count + EDGE :], bands.at[0], sd.at[0], rd.at[0], {"slab": after})
    under = launch(spread.at[:EDGE], bands.at[1], sd.at[1], rd.at[1], {"slab": before})

    remote(vset.at[:, :, other], vback, sv.at[3], rv.at[3], {"slab": mate}).wait_recv()
    mine = rel_of[:, own] >= 0
    for k in range(2):
        vout[k] = jnp.where(mine, vset[k, :, own], vback[k])

    term = None
    for h in range(2):
        for d in range(n - 1, 0, -1):
            src = flip(me, d)
            inward(h, src, src, d, src).wait_recv()
        row = jnp.concatenate([recv2[h, j] for j in range(n)], axis=0)
        more = lax.dot_general(
            row, af[h * half : (h + 1) * half, :], leading, preferred_element_type=f32
        )
        term = more if term is None else term + more
    for d in range(n - 1, 0, -1):
        src = flip(me, d)
        remote(send3.at[src], recv3.at[src], sw.at[d], rw.at[src], {"slab": src}).wait_recv()
    tails = jnp.concatenate([recv3[n - 1 - k] for k in range(side)], axis=0)
    term = term + lax.dot_general(tails, edge[...], leading, preferred_element_type=f32)
    over.wait_recv()
    under.wait_recv()
    wave_first = spread[EDGE : 2 * EDGE, :] + jnp.where(me > 0, bands[0], 0.0)
    wave_last = spread[count : count + EDGE, :] + jnp.where(me < n - 1, bands[1], 0.0)
    wave = jnp.concatenate(
        [wave_first, spread[2 * EDGE : count, :], wave_last], axis=0
    )
    out[...] = jnp.maximum(img[...] - tau_step * (term + wave), 0.0)

    for copy in sends:
        copy.wait_send()


def local_kernel(n, c, image, margin, cells, weights, observed, dual_start):
    count, width = image.shape[1], image.shape[2]
    vis = cells.shape[1]
    tall = count + 2 * EDGE
    part, half = count // 2, width // 2
    half_t, f32 = jnp.bfloat16, jnp.float32
    V = pltpu.VMEM
    dma = pltpu.SemaphoreType.DMA
    row_map = wide_row_map(count)
    vm = pl.BlockSpec(memory_space=pltpu.VMEM)
    anywhere = pl.BlockSpec(memory_space=pl.ANY)
    fresh, dual = pl.pallas_call(
        functools.partial(whole_kernel, n, c),
        out_shape=(
            jax.ShapeDtypeStruct((count, width), f32),
            jax.ShapeDtypeStruct((2, 1, vis), f32),
        ),
        in_specs=[anywhere] * 12,
        out_specs=(vm, vm),
        scratch_shapes=[
            pltpu.SMEM((1,), jnp.int32),
            V((count, width), f32),
            V((2, 1, vis), f32),
            V((2, 1, vis), f32),
            V((n // 2 * TILE, width), half_t),
            V((2, 4 * LANES, 2 * LANES), half_t),
            V((2, 6 * LANES, 2 * LANES), half_t),
            V((tall, count), f32),
            V((count, tall), f32),
            dma((12,)),
            V((width, width), half_t),
            V((width, width), half_t),
            V((half, 2 * vis), half_t),
            V((2 * count, 2 * vis), half_t),
            V((1, 2 * vis), jnp.int32),
            V((1, 2 * vis), f32),
            V((2, 1, 2 * vis), f32),
            V((2, 1, 2 * vis), f32),
            V((2, 1, vis), f32),
            V((1, 2 * vis), jnp.int32),
            V((1, 2 * vis), jnp.int32),
            V((1, 2 * vis), jnp.int32),
            V((half // 2, 2 * vis), half_t),
            V((2, n, part + TILE, count), half_t),
            V((2, n, part + TILE, count), half_t),
            V((2, n, part, count), half_t),
            V((2, n, part, count), half_t),
            V((n, TILE, count), half_t),
            V((n, TILE, count), half_t),
            V((2 * count, half), half_t),
            V((width, width), half_t),
            V((tall, width + 2 * LANES), f32),
            V((2, EDGE, width), f32),
            V((count, width), f32),
            V((count, width), half_t),
            V((c, count, width // c), half_t),
            V((c, count, width // c), half_t),
            V((count, width + 4 * LANES), f32),
            V((tall, width), f32),
            V((2, EDGE, width), f32),
            dma((2, n)), dma((2, n)), dma((2, n)), dma((2, n)), dma((2,)), dma((2,)),
            dma((c,)), dma((c,)), dma((c,)), dma((c,)), dma((2,)), dma((2,)),
            dma((4,)), dma((4,)), dma((n,)), dma((n,)),
        ],
        compiler_params=pltpu.CompilerParams(
            collective_id=0, has_side_effects=True, vmem_limit_bytes=60 * 1024 * 1024
        ),
    )(
        image[0], margin, cells, weights, observed, dual_start,
        owner_table(n, count, width), edge_table(n, count, width),
        in_two(analysis_map()), in_two(synthesis_map()),
        row_map, np.ascontiguousarray(row_map.T),
    )
    return (fresh[None], dual)


def solution(mesh):
    n, c = mesh.shape["slab"], mesh.shape["chan"]

    def local(image, *rest):
        count, width = image.shape[1], image.shape[2]
        fits = n == 8 and count == LANES and width == n * count and width % (c * LANES) == 0
        if fits and rest[1].shape[1] % CHUNK == 0:
            return local_kernel(n, c, image, *rest)
        return local_plain(image, *rest)

    in_specs = (
        P("chan", "slab", None),
        P("slab"),
        P("chan", "slab"),
        P("chan", "slab"),
        P(None, "chan", "slab"),
        P(None, "chan", "slab"),
    )
    out_specs = (P("chan", "slab", None), P(None, "chan", "slab"))
    return jax.shard_map(local, mesh=mesh, in_specs=in_specs, out_specs=out_specs, check_vma=False)
```

```python
import functools
import math

import jax
import jax.numpy as jnp
import numpy as np
from jax import lax
from jax.experimental import pallas as pl
from jax.experimental.pallas import tpu as pltpu
from jax.sharding import PartitionSpec as P

N = 1024
HALO = 3


low_taps = (
    -0.010597401784997278,
    0.032883011666982945,
    0.030841381835986965,
    -0.18703481171888114,
    -0.02798376941698385,
    0.6308807679295904,
    0.7148465705525415,
    0.23037781330885523,
)
high_taps = (
    -0.23037781330885523,
    0.7148465705525415,
    -0.6308807679295904,
    -0.02798376941698385,
    0.18703481171888114,
    0.030841381835986965,
    -0.032883011666982945,
    -0.010597401784997278,
)
tau_step = 0.5
bound_level = 3.0
leading = (((0,), (0,)), ((), ()))


def with_halo(block, sides, width):
    for axis, dim in sides:
        count = lax.axis_size(axis)
        forward = [(i, i + 1) for i in range(count - 1)]
        backward = [(target, source) for source, target in forward]
        low = lax.ppermute(
            lax.slice_in_dim(block, block.shape[dim] - width, None, axis=dim), axis, forward
        )
        high = lax.ppermute(lax.slice_in_dim(block, 0, width, axis=dim), axis, backward)
        block = jnp.concatenate([low, block, high], axis=dim)
    return block


def tap_value(offset, taps):
    total = jnp.zeros(offset.shape, jnp.float32)
    for position in range(8):
        total = total + jnp.where(offset == position, taps[position], 0.0).astype(jnp.float32)
    return total


def fourier_tables(length):
    index = jnp.arange(length, dtype=jnp.int32)
    product = index[:, None] * index[None, :] % length
    angle = product.astype(jnp.float32) * (2.0 * math.pi / length)
    scale = 1.0 / math.sqrt(length)
    return (
        (jnp.cos(angle) * scale).astype(jnp.bfloat16),
        (jnp.sin(angle) * scale).astype(jnp.bfloat16),
    )


def row_matrix(count):
    half = count // 2
    line = jnp.arange(count + 2 * HALO, dtype=jnp.int32)[:, None]
    column = jnp.arange(count, dtype=jnp.int32)[None, :]
    offset = line - 2 * (column % half)
    return jnp.where(column < half, tap_value(offset, low_taps), tap_value(offset, high_taps))


def facet_mask(count, width):
    line = jnp.arange(count + 2 * HALO, dtype=jnp.int32)
    distance = jnp.maximum(jnp.maximum(HALO - line, line - count - HALO + 1), 0)
    return (distance[None, :] <= width[:, None]).astype(jnp.float32)


def column_forward(values):
    width = values.shape[1]
    half = width // 2
    padded = jnp.pad(values, ((0, 0), (HALO, 8)))
    even_cells = padded[:, 0::2]
    odd_cells = padded[:, 1::2]
    low_part = jnp.zeros((values.shape[0], half), jnp.float32)
    high_part = jnp.zeros((values.shape[0], half), jnp.float32)
    for position in range(8):
        source = even_cells if position % 2 == 0 else odd_cells
        piece = source[:, position // 2 : position // 2 + half]
        low_part = low_part + low_taps[position] * piece
        high_part = high_part + high_taps[position] * piece
    return jnp.concatenate([low_part, high_part], axis=1)


def column_adjoint(coefs):
    width = coefs.shape[1]
    half = width // 2
    low_part = coefs[:, :half]
    high_part = coefs[:, half:]
    even_sums = jnp.zeros((coefs.shape[0], half + 4), jnp.float32)
    odd_sums = jnp.zeros((coefs.shape[0], half + 4), jnp.float32)
    for position in range(8):
        term = low_taps[position] * low_part + high_taps[position] * high_part
        placed = jnp.pad(term, ((0, 0), (position // 2, 4 - position // 2)))
        if position % 2 == 0:
            even_sums = even_sums + placed
        else:
            odd_sums = odd_sums + placed
    joined = jnp.stack([even_sums, odd_sums], axis=2).reshape(coefs.shape[0], width + 8)
    return joined[:, HALO : HALO + width]


def data_part(lifted, dual, seen, places, gains, cos_table, sin_table):
    flat_b = lifted.astype(jnp.bfloat16)
    spectra = jnp.stack(
        [
            jnp.dot(flat_b, cos_table, preferred_element_type=jnp.float32),
            -jnp.dot(flat_b, sin_table, preferred_element_type=jnp.float32),
        ]
    ).astype(jnp.bfloat16)
    columns = lax.all_to_all(spectra, "slab", split_axis=2, concat_axis=1, tiled=True)
    grid_real = lax.dot_general(
        columns[0], cos_table, leading, preferred_element_type=jnp.float32
    ) + lax.dot_general(columns[1], sin_table, leading, preferred_element_type=jnp.float32)
    grid_imag = lax.dot_general(
        columns[1], cos_table, leading, preferred_element_type=jnp.float32
    ) - lax.dot_general(columns[0], sin_table, leading, preferred_element_type=jnp.float32)
    model = jnp.stack(
        [gains * grid_real.reshape(-1)[places], gains * grid_imag.reshape(-1)[places]]
    )
    fresh_dual = (dual + (model - seen)) / 2.0
    weighted = gains[None, :] * fresh_dual
    cell_count = grid_real.size
    hold_real = (
        jnp.zeros((cell_count,), jnp.float32)
        .at[places]
        .add(weighted[0])
        .reshape(grid_real.shape)
        .astype(jnp.bfloat16)
    )
    hold_imag = (
        jnp.zeros((cell_count,), jnp.float32)
        .at[places]
        .add(weighted[1])
        .reshape(grid_real.shape)
        .astype(jnp.bfloat16)
    )
    backward = jnp.stack(
        [
            jnp.dot(hold_real, cos_table, preferred_element_type=jnp.float32)
            - jnp.dot(hold_imag, sin_table, preferred_element_type=jnp.float32),
            jnp.dot(hold_real, sin_table, preferred_element_type=jnp.float32)
            + jnp.dot(hold_imag, cos_table, preferred_element_type=jnp.float32),
        ]
    ).astype(jnp.bfloat16)
    returned = lax.all_to_all(backward, "slab", split_axis=2, concat_axis=1, tiled=True)
    data_term = lax.dot_general(
        returned[0], cos_table, leading, preferred_element_type=jnp.float32
    ) - lax.dot_general(returned[1], sin_table, leading, preferred_element_type=jnp.float32)
    return (data_term, fresh_dual)


def wave_part(lifted, row_map, mask):
    highest = lax.Precision.HIGHEST
    count = lifted.shape[0]
    extended = with_halo(lifted, (("slab", 0),), HALO) * mask
    filtered = column_forward(extended)
    coef = lax.dot_general(
        row_map, filtered, leading, precision=highest, preferred_element_type=jnp.float32
    )
    squares = coef * coef
    share = lax.psum_scatter(
        squares.astype(jnp.bfloat16), "chan", scatter_dimension=1, tiled=True
    ).astype(jnp.float32)
    partial_factor = bound_level / jnp.maximum(jnp.sqrt(share), bound_level)
    factor = lax.all_gather(partial_factor, "chan", axis=1, tiled=True)
    fresh_dual = coef * factor
    back = column_adjoint(fresh_dual)
    spread = jnp.dot(row_map, back, precision=highest, preferred_element_type=jnp.float32) * mask
    bands = jnp.concatenate([spread[:HALO], spread[count + HALO :]], axis=0)
    arrived = with_halo(bands, (("slab", 0),), HALO)
    inner = spread[HALO : count + HALO]
    inner = inner.at[:HALO].add(arrived[:HALO])
    inner = inner.at[count - HALO :].add(arrived[3 * HALO :])
    return (inner, fresh_dual)


def local_plain(image, margin, cells, weights, observed, dual_start):
    count = image.shape[1]
    cos_table, sin_table = fourier_tables(N)
    row_map = row_matrix(count)
    mask = facet_mask(count, margin)[0][:, None]
    places = cells[0]
    gains = weights[0]
    seen = observed[:, 0, :]
    dual = dual_start[:, 0, :]
    estimate = image[0]
    data_term, dual = data_part(estimate, dual, seen, places, gains, cos_table, sin_table)
    wave_term, wave_dual = wave_part(estimate, row_map, mask)
    fresh = jnp.maximum(estimate - tau_step * (data_term + wave_term), 0.0)
    return (fresh[None], dual[:, None, :])


LANES = 128
EDGE = 8
CHUNK = 1024
TILE = 16
highest = lax.Precision.HIGHEST
crossed = (((1,), (1,)), ((), ()))


def pick(offset, taps):
    inside = (offset >= 0) & (offset < 8)
    return np.where(inside, np.asarray(taps, np.float64)[np.clip(offset, 0, 7)], 0.0)


def both_taps(offset, is_low):
    return np.where(is_low, pick(offset, low_taps), pick(offset, high_taps)).astype(np.float32)


def wave_rows(lines, length, span):
    angle = lines[:, None] * np.arange(span)[None, :] % length * (2.0 * np.pi / length)
    scale = 1.0 / np.sqrt(length)
    return np.cos(angle) * scale, -np.sin(angle) * scale


def first_column(owner, n, count):
    return count * owner if owner < n // 2 else count * (n - 1 - owner) + count // 2


def owner_table(n, count, width):
    blocks = []
    few = count // 4
    for h in range(2):
        for owner in range(n):
            lines = first_column(owner, n, count) + h * few + np.arange(few)
            blocks.extend(wave_rows(lines, width, width // 2))
    return np.concatenate(blocks).astype(np.float32).astype(jnp.bfloat16)


def edge_table(n, count, width):
    table = np.zeros((n // 2, TILE, width), np.float32)
    real, imag = wave_rows(count * (1 + np.arange(n // 2)), width, width)
    table[:, 0], table[:, TILE // 2] = real, imag
    return table.reshape(-1, width).astype(jnp.bfloat16)


def analysis_map():
    line = np.arange(4 * LANES)[:, None]
    column = np.arange(2 * LANES)[None, :]
    offset = line - (LANES - HALO) - 2 * (column % LANES)
    return both_taps(offset, column < LANES)


def synthesis_map():
    line = np.arange(6 * LANES)[:, None]
    column = np.arange(2 * LANES)[None, :]
    block = line // (2 * LANES) - 1
    offset = column - 2 * LANES * block - 2 * (line % LANES) + HALO
    return both_taps(offset, line % (2 * LANES) < LANES)


def wide_row_map(count):
    half = count // 2
    line = np.arange(count + 2 * EDGE)[:, None] - (EDGE - HALO)
    column = np.arange(count)[None, :]
    offset = line - 2 * (column % half)
    return both_taps(offset, column < half)


def in_two(values):
    top = values.astype(jnp.bfloat16)
    return np.stack([top, (values - top.astype(np.float32)).astype(jnp.bfloat16)])


def split(value):
    top = value.astype(jnp.bfloat16)
    return top, (value - top.astype(jnp.float32)).astype(jnp.bfloat16)


def fine_dot(left, right):
    total = jnp.dot(left[0], right[0], preferred_element_type=jnp.float32)
    total = total + jnp.dot(left[1], right[0], preferred_element_type=jnp.float32)
    return total + jnp.dot(left[0], right[1], preferred_element_type=jnp.float32)


def flip(place, bits):
    result = place
    for bit in (1, 2, 4):
        if bits & bit:
            result = result + bit - 2 * bit * (place // bit % 2)
    return result


def iota(shape, dim):
    return lax.broadcasted_iota(jnp.int32, shape, dim)


def whole_kernel(
    n, c, img_far, margin_far, cells, gains, seen_far, dual_far,
    half_far, edge_far, m1_far, m2_far, rows_far, rows_t_far,
    out, vout,
    margin, img, seen, dual, edge, m1, m2, rows, rows_t, fetched,
    af, bf, hot, marks, cset, gset, dset, vset, vback, rel_of, mod_of, fold_of, warm,
    send1, recv1, send2, recv2, send3, recv3, grid, bft,
    padded, halo, coef, sq, sq_in, totals, cpad, spread, bands,
    sa, ra, sb, rb, sh, rh, ss, rs, st, rt, sd, rd, sv, rv, sw, rw,
):
    me = lax.axis_index("slab")
    ch = lax.axis_index("chan")
    count, width = img.shape
    vis = cells.shape[1]
    part, half, side, few = count // 2, width // 2, n // 2, count // 4
    tall = count + 2 * EDGE
    pair = 2 * LANES
    block = width // c
    after, before, mate = lax.rem(me + 1, n), lax.rem(me + n - 1, n), n - 1 - me
    upper = me // side
    own = pl.ds(pl.multiple_of(upper * vis, vis), vis)
    other = pl.ds(pl.multiple_of((1 - upper) * vis, vis), vis)
    f32, bf16 = jnp.float32, jnp.bfloat16

    barrier = pltpu.get_barrier_semaphore()
    for d in range(1, n):
        pl.semaphore_signal(
            barrier, inc=1, device_id={"slab": lax.rem(me + d, n)},
            device_id_type=pl.DeviceIdType.MESH,
        )
    for d in range(1, c):
        pl.semaphore_signal(
            barrier, inc=1, device_id={"chan": lax.rem(ch + d, c)},
            device_id_type=pl.DeviceIdType.MESH,
        )

    local = [
        (img_far, img), (half_far, af.at[:, :half]), (edge_far, edge),
        (cells, cset.at[:, own]), (gains, gset.at[:, own]), (seen_far, seen), (dual_far, dual),
        (margin_far, margin), (m1_far, m1), (rows_far, rows), (rows_t_far, rows_t), (m2_far, m2),
    ]
    fetches = [
        pltpu.make_async_copy(far, near, fetched.at[i]) for i, (far, near) in enumerate(local)
    ]
    for fetch in fetches:
        fetch.start()

    def remote(src, dst, s, r, where):
        return pltpu.make_async_remote_copy(
            src_ref=src, dst_ref=dst, send_sem=s, recv_sem=r, device_id=where,
            device_id_type=pl.DeviceIdType.MESH,
        )

    sends = []

    def launch(*args):
        copy = remote(*args)
        copy.start()
        sends.append(copy)
        return copy

    for fetch in fetches[:3]:
        fetch.wait()
    flip_row = (1 - 2 * (iota((count, half), 0) % 2)).astype(f32).astype(bf16)
    for j in range(n):
        here = slice(j * count, (j + 1) * count)
        af[here, half:] = af[here, :half] * flip_row

    flat_b = img[...].astype(bf16)
    send1[0, :, part:, :] = jnp.zeros((n, TILE, count), bf16)
    spec = lax.dot_general(edge[...], flat_b, crossed, preferred_element_type=f32).astype(bf16)
    for j in range(n):
        k = n - 1 - j
        send1[1, j, part:, :] = (
            spec[k * TILE : (k + 1) * TILE] if j >= side else jnp.zeros((TILE, count), bf16)
        )

    def spectra(h):
        spec = lax.dot_general(
            af[h * half : (h + 1) * half, :], flat_b, crossed, preferred_element_type=f32
        ).astype(bf16)
        for j in range(n):
            send1[h, j, :part, :] = spec[j * part : (j + 1) * part]

    def outward(h, src, peer, d, home):
        rows = part if h == 0 else part + TILE
        return remote(
            send1.at[h, src, :rows], recv1.at[h, home, :rows], sa.at[h, d], ra.at[h, home],
            {"slab": peer},
        )

    def scatter(h):
        for d in range(n - 1, 0, -1):
            peer = flip(me, d)
            copy = outward(h, peer, peer, d, me)
            copy.start()
            sends.append(copy)
        recv1[h, me] = send1[h, me]

    fetches[3].wait()
    spectra(0)
    spectra(1)
    pl.semaphore_wait(barrier, n + c - 2)
    launch(cset.at[:, own], cset.at[:, own], sv.at[0], rv.at[0], {"slab": mate})
    up = launch(img.at[count - EDGE :], halo.at[0], sh.at[0], rh.at[0], {"slab": after})
    down = launch(img.at[:EDGE], halo.at[1], sh.at[1], rh.at[1], {"slab": before})
    scatter(0)
    scatter(1)
    for fetch in fetches[4:7]:
        fetch.wait()
    dset[:, :, own] = dual[...] - seen[...]
    launch(gset.at[:, own], gset.at[:, own], sv.at[1], rv.at[1], {"slab": mate})
    launch(dset.at[:, :, own], dset.at[:, :, own], sv.at[2], rv.at[2], {"slab": mate})

    def locate(here, sign):
        spot = cset[:, here]
        column, line = spot // width, spot % width
        column = jnp.where(sign > 0, column, count - column) - part * upper
        line = jnp.where((sign > 0) | (line == 0), line, width - line)
        rel_of[:, here] = jnp.where(column >= part + upper, -1, column)
        mod_of[:, here] = line
        fold = jnp.where(line > half, width - line, jnp.where(line == half, 0, line))
        fold_of[:, here] = fold

    step = 32

    def heat(here):
        fold = fold_of[:, here]

        def body(i, carry):
            hit = jnp.where(iota((step, vis), 0) + i * step == fold, 1.0, 0.0).astype(bf16)
            hot[pl.ds(pl.multiple_of(i * step, step), step), here] = hit
            return carry

        lax.fori_loop(0, half // step, body, 0)

        def merge(i, carry):
            top = pl.ds(pl.multiple_of(i * step, step), step)
            low = pl.ds(pl.multiple_of(half // 2 + i * step, step), step)
            warm[top, here] = hot[top, here] + hot[low, here]
            return carry

        lax.fori_loop(0, half // 2 // step, merge, 0)

    locate(own, 1 - 2 * upper)
    heat(own)


    for fetch in fetches[7:]:
        fetch.wait()
    reach = margin[0]

    def keep(shape, dim):
        line = iota(shape, dim)
        distance = jnp.maximum(jnp.maximum(EDGE - line, line - count - EDGE + 1), 0)
        return jnp.where(distance <= reach, 1.0, 0.0)

    row_fwd = split(rows_t[...] * keep((count, tall), 1))
    row_adj = split(rows[...] * keep((tall, count), 0))

    flip_lane = (1 - 2 * (iota((few, half), 1) % 2)).astype(f32).astype(bf16)
    nyquist = (1 - 2 * (iota((few, LANES), 0) % 2)).astype(f32) * (1.0 / math.sqrt(width))
    first_lane = iota((few, LANES), 1) == 0
    for j in range(2 * n):
        top = first_column(j % n, n, count) + j // n * few
        cosine = af[j * part : j * part + few, :half]
        sine = -af[j * part + few : (j + 1) * part, :half]
        mixed = jnp.where(first_lane, nyquist, sine[:, :LANES].astype(f32)).astype(bf16)
        for low, value in ((top, None), (half + top, flip_lane)):
            here = slice(low, low + few)
            bf[here, :half] = cosine if value is None else cosine * value
            rest = sine if value is None else sine * value
            bf[here, half : half + LANES] = (
                mixed if value is None else mixed * value[:, :LANES]
            )
            bf[here, half + LANES :] = rest[:, LANES:]
        bft[top : top + few, :] = af[j * part : j * part + few, :]
        bft[half + top : half + top + few, :] = -af[j * part + few : (j + 1) * part, :]
    pole = (1 - 2 * (iota((TILE, width), 1) % 2)).astype(f32) * (1.0 / math.sqrt(width))
    first_row = iota((TILE, width), 0) == 0
    bft[half : half + TILE, :] = jnp.where(
        first_row, pole, bft[half : half + TILE, :].astype(f32)
    ).astype(bf16)

    padded[:, :LANES] = jnp.zeros((tall, LANES), f32)
    padded[:, LANES + width :] = jnp.zeros((tall, LANES), f32)
    padded[EDGE : EDGE + count, LANES : LANES + width] = img[...]
    up.wait_recv()
    down.wait_recv()
    padded[:EDGE, LANES : LANES + width] = jnp.where(me > 0, halo[0], 0.0)
    padded[EDGE + count :, LANES : LANES + width] = jnp.where(me < n - 1, halo[1], 0.0)
    for b in range(width // pair):
        filtered = fine_dot(split(padded[:, b * pair : b * pair + 4 * LANES]), m1)
        piece = fine_dot(row_fwd, split(filtered))
        coef[:, b * pair : (b + 1) * pair] = piece
        sq[:, b * pair : (b + 1) * pair] = (piece * piece).astype(bf16)

    def slot(who):
        return pl.ds(pl.multiple_of(who * block, block), block)

    for d in range(1, c):
        peer = lax.rem(ch + d, c)
        launch(sq.at[:, slot(peer)], sq_in.at[ch], ss.at[d], rs.at[ch], {"chan": peer})

    remote(cset.at[:, other], cset.at[:, other], sv.at[0], rv.at[0], {"slab": mate}).wait_recv()
    locate(other, 2 * upper - 1)
    heat(other)

    def arrive(h):
        for d in range(n - 1, 0, -1):
            src = flip(me, d)
            outward(h, src, src, d, src).wait_recv()
        rows = part if h == 0 else part + TILE
        columns = jnp.concatenate([recv1[h, j, :rows] for j in range(n)], axis=1)
        value = jnp.dot(columns, bf[...], preferred_element_type=f32)
        planes = []
        for lanes in (slice(0, half), slice(half, width)):
            for k in range(2):
                planes.append(value[k * few : (k + 1) * few, lanes])
                if h == 1:
                    planes.append(value[part + k * EDGE : part + (k + 1) * EDGE, lanes])
        rows = sum(plane.shape[0] for plane in planes)
        grid[:rows] = jnp.concatenate(planes, axis=0).astype(bf16)

    def factors(line, sign):
        even = jnp.where(line == half, 0.0, 1.0)
        odd = jnp.where(line > half, -1.0, 1.0)
        odd = jnp.where((line == half) | (line == 0), 0.0, odd)
        return even, odd, 1.0 - even

    def spread_out(line, gain, fresh, sign):
        even, odd, last = factors(line, sign)
        real, imag = gain * fresh[0], gain * fresh[1] * sign
        return even * real, even * imag, last * real - odd * imag, odd * real + last * imag

    def visit(h, base, sign, i, carry):
        here = pl.ds(pl.multiple_of(base * vis + i * CHUNK, CHUNK), CHUNK)
        deep = few + h * EDGE
        found = jnp.dot(grid[: 4 * deep], hot[:, here], preferred_element_type=f32)
        rel = rel_of[:, here] - h * few
        match = iota((deep, CHUNK), 0) == rel
        c_re, c_im, s_re, s_im = [
            jnp.sum(
                jnp.where(match, found[k * deep : (k + 1) * deep], 0.0), axis=0, keepdims=True
            )
            for k in range(4)
        ]
        line = mod_of[:, here]
        gain = gset[:, here]
        even, odd, last = factors(line, sign)
        real = even * c_re + odd * s_im + last * s_re
        imag = (even * c_im - odd * s_re + last * s_im) * sign
        fresh = []
        for k, model in enumerate((real, imag)):
            fresh.append((dset[k, :, here] + gain * model) / 2.0)
            vset[k, :, here] = (
                fresh[k] if h == 0 else jnp.where(rel >= 0, fresh[k], vset[k, :, here])
            )
        late = fold_of[:, here] >= half // 2
        values = spread_out(line, gain, fresh, sign)
        for v in range(2):
            near = iota((few, CHUNK), 0) == jnp.where(late == (v == 1), rel, -1)
            for k, mark in enumerate(values):
                low = (v * 4 + k) * few
                marks[low : low + few, here] = jnp.where(near, mark, 0.0).astype(bf16)
        return carry

    facing = (1 - 2 * upper).astype(f32)
    def inward(h, src, peer, d, home):
        return remote(
            send2.at[h, src], recv2.at[h, home], sb.at[h, d], rb.at[h, home], {"slab": peer}
        )

    def give(h, bits):
        for d in bits:
            peer = flip(me, d)
            copy = inward(h, peer, peer, d, me)
            copy.start()
            sends.append(copy)

    for h in range(2):
        arrive(h)
        if h == 0:
            here_first = functools.partial(visit, h, upper, facing)
            lax.fori_loop(0, vis // CHUNK, here_first, 0, unroll=2)
            for d in range(1, c):
                src = lax.rem(ch + d, c)
                remote(sq.at[:, slot(src)], sq_in.at[src], ss.at[d], rs.at[src], {"chan": src}).wait_recv()
            total = sq[:, slot(ch)].astype(f32)
            for d in range(1, c):
                total = total + sq_in[lax.rem(ch + d, c)].astype(f32)
            totals[ch] = total.astype(bf16)
            for d in range(1, c):
                peer = lax.rem(ch + d, c)
                launch(totals.at[ch], totals.at[ch], st.at[d], rt.at[ch], {"chan": peer})
            remote(
                gset.at[:, other], gset.at[:, other], sv.at[1], rv.at[1], {"slab": mate}
            ).wait_recv()
            remote(
                dset.at[:, :, other], dset.at[:, :, other], sv.at[2], rv.at[2], {"slab": mate}
            ).wait_recv()
        else:
            here_first = functools.partial(visit, h, upper, facing)
            lax.fori_loop(0, vis // CHUNK, here_first, 0, unroll=2)
        there = functools.partial(visit, h, 1 - upper, -facing)
        lax.fori_loop(0, vis // CHUNK, there, 0, unroll=2)
        if h == 1:
            launch(vset.at[:, :, other], vback, sv.at[3], rv.at[3], {"slab": mate})
        held = lax.dot_general(
            marks[...], warm[...], crossed, preferred_element_type=f32
        ).astype(bf16)
        quarters = [held[low : low + part] for low in (0, count, part, count + part)]
        back = jnp.dot(
            jnp.concatenate(quarters, axis=1), bft[...], preferred_element_type=f32
        ).astype(bf16)
        for j in range(n):
            send2[h, j] = back[:, j * count : (j + 1) * count]
        give(h, range(n - 1, 0, -1))
        recv2[h, me] = send2[h, me]

    coarse, fine = half // 32, 32

    def outer(i, carry):
        here = pl.ds(pl.multiple_of(vis + i * CHUNK, CHUNK), CHUNK)
        line = mod_of[:, here]
        fold = jnp.where(line > half, width - line, jnp.where(line == half, 0, line))
        fresh = [vset[0, :, here], vset[1, :, here]]
        left = jnp.where(iota((coarse, CHUNK), 0) == fold // fine, 1.0, 0.0).astype(bf16)
        match = (iota((fine, CHUNK), 0) == fold % fine) & (rel_of[:, here] == part)
        right = jnp.concatenate(
            [
                jnp.where(match, mark, 0.0).astype(bf16)
                for mark in spread_out(line, gset[:, here], fresh, -1.0)
            ],
            axis=0,
        )
        return carry + lax.dot_general(right, left, crossed, preferred_element_type=f32)

    edges = lax.fori_loop(0, vis // CHUNK, outer, jnp.zeros((4 * fine, coarse), f32))
    lane = iota((coarse, half), 1)
    grow = jnp.where(lane // fine == iota((coarse, half), 0), 1.0, 0.0).astype(bf16)
    grown = jnp.dot(edges.astype(bf16), grow, preferred_element_type=f32)
    lane, line = iota((4 * fine, half), 1), iota((4 * fine, half), 0)
    grown = jnp.where(lane % fine == line % fine, grown, 0.0).astype(bf16)
    line, lane = iota((TILE, 4 * fine), 0), iota((TILE, 4 * fine), 1) // fine
    rows_of = []
    for k in range(2):
        gather = jnp.where(line == EDGE * (lane - 2 * k), 1.0, 0.0).astype(bf16)
        rows_of.append(jnp.dot(gather, grown, preferred_element_type=f32).astype(bf16))
    tails = jnp.dot(
        jnp.concatenate(rows_of, axis=1), bft[...], preferred_element_type=f32
    ).astype(bf16)
    for j in range(n):
        send3[j] = tails[:, j * count : (j + 1) * count]
    for d in range(n - 1, 0, -1):
        peer = flip(me, d)
        launch(send3.at[peer], recv3.at[me], sw.at[d], rw.at[me], {"slab": peer})
    recv3[me] = send3[me]

    for d in range(1, c):
        src = lax.rem(ch + d, c)
        remote(totals.at[src], totals.at[src], st.at[d], rt.at[src], {"chan": src}).wait_recv()
    cpad[:, :pair] = jnp.zeros((count, pair), f32)
    cpad[:, pair + width :] = jnp.zeros((count, pair), f32)
    for j in range(c):
        here = slice(j * block, (j + 1) * block)
        factor = bound_level / jnp.maximum(jnp.sqrt(totals[j].astype(f32)), bound_level)
        cpad[:, pair + j * block : pair + (j + 1) * block] = coef[:, here] * factor
    for b in range(width // pair):
        near = cpad[:, b * pair : b * pair + 6 * LANES].astype(bf16)
        back = jnp.dot(near, m2[0], preferred_element_type=f32)
        back = back + jnp.dot(near, m2[1], preferred_element_type=f32)
        back_b = back.astype(bf16)
        spread[:, b * pair : (b + 1) * pair] = jnp.dot(
            row_adj[0], back_b, preferred_element_type=f32
        ) + jnp.dot(row_adj[1], back_b, preferred_element_type=f32)
    over = launch(spread.at[count + EDGE :], bands.at[0], sd.at[0], rd.at[0], {"slab": after})
    under = launch(spread.at[:EDGE], bands.at[1], sd.at[1], rd.at[1], {"slab": before})

    remote(vset.at[:, :, other], vback, sv.at[3], rv.at[3], {"slab": mate}).wait_recv()
    mine = rel_of[:, own] >= 0
    for k in range(2):
        vout[k] = jnp.where(mine, vset[k, :, own], vback[k])

    term = None
    for h in range(2):
        for d in range(n - 1, 0, -1):
            src = flip(me, d)
            inward(h, src, src, d, src).wait_recv()
        row = jnp.concatenate([recv2[h, j] for j in range(n)], axis=0)
        more = lax.dot_general(
            row, af[h * half : (h + 1) * half, :], leading, preferred_element_type=f32
        )
        term = more if term is None else term + more
    for d in range(n - 1, 0, -1):
        src = flip(me, d)
        remote(send3.at[src], recv3.at[src], sw.at[d], rw.at[src], {"slab": src}).wait_recv()
    tails = jnp.concatenate([recv3[n - 1 - k] for k in range(side)], axis=0)
    term = term + lax.dot_general(tails, edge[...], leading, preferred_element_type=f32)
    over.wait_recv()
    under.wait_recv()
    wave_first = spread[EDGE : 2 * EDGE, :] + jnp.where(me > 0, bands[0], 0.0)
    wave_last = spread[count : count + EDGE, :] + jnp.where(me < n - 1, bands[1], 0.0)
    wave = jnp.concatenate(
        [wave_first, spread[2 * EDGE : count, :], wave_last], axis=0
    )
    out[...] = jnp.maximum(img[...] - tau_step * (term + wave), 0.0)

    for copy in sends:
        copy.wait_send()


def local_kernel(n, c, image, margin, cells, weights, observed, dual_start):
    count, width = image.shape[1], image.shape[2]
    vis = cells.shape[1]
    tall = count + 2 * EDGE
    part, half = count // 2, width // 2
    half_t, f32 = jnp.bfloat16, jnp.float32
    V = pltpu.VMEM
    dma = pltpu.SemaphoreType.DMA
    row_map = wide_row_map(count)
    vm = pl.BlockSpec(memory_space=pltpu.VMEM)
    anywhere = pl.BlockSpec(memory_space=pl.ANY)
    fresh, dual = pl.pallas_call(
        functools.partial(whole_kernel, n, c),
        out_shape=(
            jax.ShapeDtypeStruct((count, width), f32),
            jax.ShapeDtypeStruct((2, 1, vis), f32),
        ),
        in_specs=[anywhere] * 12,
        out_specs=(vm, vm),
        scratch_shapes=[
            pltpu.SMEM((1,), jnp.int32),
            V((count, width), f32),
            V((2, 1, vis), f32),
            V((2, 1, vis), f32),
            V((n // 2 * TILE, width), half_t),
            V((2, 4 * LANES, 2 * LANES), half_t),
            V((2, 6 * LANES, 2 * LANES), half_t),
            V((tall, count), f32),
            V((count, tall), f32),
            dma((12,)),
            V((width, width), half_t),
            V((width, width), half_t),
            V((half, 2 * vis), half_t),
            V((2 * count, 2 * vis), half_t),
            V((1, 2 * vis), jnp.int32),
            V((1, 2 * vis), f32),
            V((2, 1, 2 * vis), f32),
            V((2, 1, 2 * vis), f32),
            V((2, 1, vis), f32),
            V((1, 2 * vis), jnp.int32),
            V((1, 2 * vis), jnp.int32),
            V((1, 2 * vis), jnp.int32),
            V((half // 2, 2 * vis), half_t),
            V((2, n, part + TILE, count), half_t),
            V((2, n, part + TILE, count), half_t),
            V((2, n, part, count), half_t),
            V((2, n, part, count), half_t),
            V((n, TILE, count), half_t),
            V((n, TILE, count), half_t),
            V((2 * count, half), half_t),
            V((width, width), half_t),
            V((tall, width + 2 * LANES), f32),
            V((2, EDGE, width), f32),
            V((count, width), f32),
            V((count, width), half_t),
            V((c, count, width // c), half_t),
            V((c, count, width // c), half_t),
            V((count, width + 4 * LANES), f32),
            V((tall, width), f32),
            V((2, EDGE, width), f32),
            dma((2, n)), dma((2, n)), dma((2, n)), dma((2, n)), dma((2,)), dma((2,)),
            dma((c,)), dma((c,)), dma((c,)), dma((c,)), dma((2,)), dma((2,)),
            dma((4,)), dma((4,)), dma((n,)), dma((n,)),
        ],
        compiler_params=pltpu.CompilerParams(
            collective_id=0, has_side_effects=True, vmem_limit_bytes=60 * 1024 * 1024
        ),
    )(
        image[0], margin, cells, weights, observed, dual_start,
        owner_table(n, count, width), edge_table(n, count, width),
        in_two(analysis_map()), in_two(synthesis_map()),
        row_map, np.ascontiguousarray(row_map.T),
    )
    return (fresh[None], dual)


def solution(mesh):
    n, c = mesh.shape["slab"], mesh.shape["chan"]

    def local(image, *rest):
        count, width = image.shape[1], image.shape[2]
        fits = n == 8 and count == LANES and width == n * count and width % (c * LANES) == 0
        if fits and rest[1].shape[1] % CHUNK == 0:
            return local_kernel(n, c, image, *rest)
        return local_plain(image, *rest)

    in_specs = (
        P("chan", "slab", None),
        P("slab"),
        P("chan", "slab"),
        P("chan", "slab"),
        P(None, "chan", "slab"),
        P(None, "chan", "slab"),
    )
    out_specs = (P("chan", "slab", None), P(None, "chan", "slab"))
    return jax.shard_map(local, mesh=mesh, in_specs=in_specs, out_specs=out_specs, check_vma=False)
```
